32 devices in a mesh: row: 8 (over y, x, core), col: 4 (over z).
Axes of the slice: x: 2, y: 2, z: 4, core: 2. Of those that a mesh axis runs over, the one named last changes fastest.
Arguments:
- offsets: float32 [2, 4, 512, 512], P(None, None, 'row', 'col'), may hold values from 0 to 1
- velocity: float32 [2, 4, 512, 512], P(None, None, 'row', 'col'), may hold values from -5 to 5
- mass: float32 [4, 512, 512], P(None, 'row', 'col'), may hold values from 0.5 to 2
- counts: int32 [512, 512], P('row', 'col'), may hold values from 0 to 4
- spectrum_low: float32 [1], replicated, may hold values from 0.5 to 2
- spectrum_high: float32 [1], replicated, may hold values from 10 to 20
Outputs:
- new_velocity: float32 [2, 4, 512, 512], P(None, None, 'row', 'col')
- pressure: float32 [4, 512, 512], P(None, 'row', 'col')
The draws below stay inside these ranges and needn't reach their ends.
Inputs may be any that keep to these rules, and one draw needn't show every extreme that they name: `counts`: slot s of a cell holds a live particle exactly when s is below the cell's count.
All inputs are finite; a program needn't handle non-finite values.
Results may differ from the reference program's by a relative error of at most 0.0001.
Values sent between devices are 32-bit elements; how exact they have to be, the bound alone decides.
A program may use at most 64 MiB of HBM per device.

```python
import math
import jax
import jax.numpy as jnp
from jax import lax

SLOTS = 4
GRID_ROWS = 512
GRID_COLS = 512


def place_ends(values, key, low, high):
    place = [jax.random.randint(jax.random.fold_in(key, axis), (), 0, length) for axis, length in enumerate(values.shape)]
    widest = values.shape.index(max(values.shape))
    next_to = place[:widest] + [(place[widest] + 1) % values.shape[widest]] + place[widest + 1:]
    return values.at[tuple(place)].set(low).at[tuple(next_to)].set(high)


def block_scale(stream_key, dims, split, smallest, largest):
    loudness = 1.0
    for position, blocks in split:
        draws = jax.random.uniform(jax.random.fold_in(jax.random.fold_in(stream_key, 6), position), (blocks,), jnp.float32, smallest / len(split), largest / len(split))
        loudness = loudness * jnp.repeat(jnp.exp(draws), dims[position] // blocks).reshape((-1,) + (1,) * (len(dims) - 1 - position))
    return loudness


def scatter_about(stream_key, shape, spread, most, shards=(), held_as=jnp.bfloat16):
    result = spread * jax.random.normal(stream_key, shape, jnp.float32)
    if shards:
        result = result * block_scale(stream_key, shape, shards, -0.22, 0.18)
    return jnp.clip(result, -most, most).astype(held_as)


def setup_inputs(seed: int = 0) -> dict:
    streams_of = jax.random.split(jax.random.key(seed), 7)
    return {
        "offsets": jnp.clip(1.0 * jax.random.uniform(streams_of[0], (2, SLOTS, GRID_ROWS, GRID_COLS), jnp.float32) ** block_scale(streams_of[0], (2, SLOTS, GRID_ROWS, GRID_COLS), ((2, 8), (3, 4)), -0.2, 0.2), 0.0, 1.0),
        "velocity": scatter_about(streams_of[1], (2, SLOTS, GRID_ROWS, GRID_COLS), 1.0, 5.0, ((2, 8), (3, 4)), jnp.float32),
        "mass": jnp.clip(jnp.exp(math.log(2.0) - 1.3862944 * jax.random.uniform(streams_of[2], (SLOTS, GRID_ROWS, GRID_COLS), jnp.float32) ** block_scale(streams_of[2], (SLOTS, GRID_ROWS, GRID_COLS), ((1, 8), (2, 4)), -0.2, 0.2)), 0.5, 2.0),
        "counts": place_ends(jax.random.randint(streams_of[3], (GRID_ROWS, GRID_COLS), 0, SLOTS + 1), jax.random.fold_in(streams_of[3], 1), 0, SLOTS).astype(jnp.int32),
        "spectrum_low": jnp.clip(jax.random.uniform(streams_of[4], (1,), jnp.float32, 0.5, 2.0), 0.5, 2.0),
        "spectrum_high": jnp.clip(jax.random.uniform(streams_of[5], (1,), jnp.float32, 10.0, 20.0), 10.0, 20.0),
    }


TIME_STEP = 0.1
SUPPORT = 2.0
KERNEL_NORM = 7.0 / (4.0 * math.pi)
SLOPE_NORM = 20.0 * KERNEL_NORM / 4.0
BACKGROUND = 0.5 * KERNEL_NORM
DIAGONAL_SHIFT = 1.0

def pair_sums(own_off, own_values, pad_off, pad_mass, pad_values, combine):
    height = own_off.shape[-2]
    breadth = own_off.shape[-1]
    totals = None
    for shift_row in range(-2, 3):
        for shift_col in range(-2, 3):

            def nearby(array):
                return array[..., 2 + shift_row:2 + shift_row + height, 2 + shift_col:2 + shift_col + breadth]
            near_off = nearby(pad_off)
            along_row = shift_row + near_off[0][None] - own_off[0][:, None]
            along_col = shift_col + near_off[1][None] - own_off[1][:, None]
            distance = jnp.sqrt(along_row * along_row + along_col * along_col)
            remain = jnp.maximum(1.0 - distance / SUPPORT, 0.0)
            masses = nearby(pad_mass)[None]
            kernel = masses * KERNEL_NORM * remain ** 4 * (1.0 + 4.0 * distance / SUPPORT)
            slopes = masses * SLOPE_NORM * remain ** 3
            pieces = combine(kernel, slopes, along_row, along_col, own_values[:, :, None], nearby(pad_values)[:, None])
            pieces = tuple((lax.optimization_barrier(jnp.sum(piece, axis=1)) for piece in pieces))
            totals = pieces if totals is None else tuple((left + right for left, right in zip(totals, pieces)))
    return totals

def flow_terms(kernel, slopes, along_row, along_col, own_values, near_values):
    inflow = (near_values[0] - own_values[0]) * along_row + (near_values[1] - own_values[1]) * along_col
    return (kernel, slopes * inflow)

def laplace_terms(kernel, slopes, along_row, along_col, own_values, near_values):
    return (slopes * (own_values[0] - near_values[0]),)

def gradient_terms(kernel, slopes, along_row, along_col, own_values, near_values):
    differ = near_values[0] - own_values[0]
    return (slopes * differ * along_row, slopes * differ * along_col)

def widen(array):
    return jnp.pad(array, [(0, 0)] * (array.ndim - 2) + [(2, 2), (2, 2)])

def by_rows(action, owns, pads):
    height = owns[0].shape[-2]
    block = math.gcd(height, 8)

    def single_block(number):
        begin_row = number * block
        own_part = tuple((lax.dynamic_slice_in_dim(array, begin_row, block, array.ndim - 2) for array in owns))
        pad_part = tuple((lax.dynamic_slice_in_dim(array, begin_row, block + 4, array.ndim - 2) for array in pads))
        return action(own_part, pad_part)
    stacked = lax.map(single_block, jnp.arange(height // block, dtype=jnp.int32))
    return tuple((jnp.moveaxis(piece, 0, -3).reshape(piece.shape[1:-2] + (height, piece.shape[-1])) for piece in stacked))

def reference(offsets, velocity, mass, counts, spectrum_low, spectrum_high):
    slot_index = lax.broadcasted_iota(jnp.int32, mass.shape, 0)
    occupied = (slot_index < counts[None]).astype(jnp.float32)
    drifted = offsets + TIME_STEP * velocity
    weight = mass * occupied
    pad_off = widen(drifted)
    pad_mass = widen(weight)
    pad_vel = widen(velocity)

    def flow_action(owns, pads):
        return pair_sums(owns[0], owns[1], pads[0], pads[1], pads[2], flow_terms)
    dens_sum, inflow = by_rows(flow_action, (drifted, velocity), (pad_off, pad_mass, pad_vel))
    density = BACKGROUND + dens_sum
    source = -inflow / (density * TIME_STEP)

    def laplace_action(owns, pads):
        return pair_sums(owns[0], owns[1], pads[0], pads[1], pads[2], laplace_terms)

    def operate(field):
        summed, = by_rows(laplace_action, (drifted, field[None]), (pad_off, pad_mass, widen(field[None])))
        return DIAGONAL_SHIFT * field + 2.0 * summed / density
    lowest = spectrum_low[0]
    highest = spectrum_high[0]
    middle = 0.5 * (highest + lowest)
    radius = 0.5 * (highest - lowest)
    quotient = middle / radius
    factor_zero = 1.0 / quotient
    first = source / middle
    residual = source - operate(first)
    factor_one = 1.0 / (2.0 * quotient - factor_zero)
    second = factor_one * factor_zero * first + 2.0 * factor_one / radius * residual
    residual = residual - operate(second)
    factor_two = 1.0 / (2.0 * quotient - factor_one)
    third = factor_two * factor_one * second + 2.0 * factor_two / radius * residual
    solved = first + second + third

    def gradient_action(owns, pads):
        return pair_sums(owns[0], owns[1], pads[0], pads[1], pads[2], gradient_terms)
    push_rows, push_cols = by_rows(gradient_action, (drifted, solved[None]), (pad_off, pad_mass, widen(solved[None])))
    push = jnp.stack([push_rows, push_cols], axis=0)
    new_velocity = occupied[None] * (velocity - TIME_STEP * push / density[None])
    return (new_velocity, occupied * solved)
```

```python
import functools
import math

import jax
import jax.numpy as jnp
from jax import lax
from jax.experimental import pallas as pl
from jax.experimental.pallas import tpu as pltpu
from jax.sharding import PartitionSpec as P

TIME_STEP = 0.1
KERNEL_NORM = 7.0 / (4.0 * math.pi)
SLOPE_NORM = 20.0 * KERNEL_NORM / 4.0
BACKGROUND = 0.5 * KERNEL_NORM
DIAGONAL_SHIFT = 1.0
TINY = 1e-30
VMEM_BYTES = 67_043_328
SPARE = 8192
MESH = pl.DeviceIdType.MESH
DIRECTIONS = ((1, 0), (-1, 0), (0, 1), (0, -1), (1, 1), (-1, 1), (1, -1), (-1, -1))


def kernel(
    rows,
    cols,
    off_hbm,
    vel_hbm,
    mass_hbm,
    counts_hbm,
    low_hbm,
    high_hbm,
    nv_ref,
    press_ref,
    off_ref,
    vel_ref,
    mass_ref,
    counts_ref,
    low_ref,
    high_ref,
    sums_ref,
    input_sem,
    state_e,
    state_cs,
    state_cr,
    field_e,
    field_cs,
    field_cr,
    near_s,
    near_p,
    slopes_ref,
    own_ref,
    send_sem,
    recv_sem,
):
    slots, height, width = mass_hbm.shape
    steps = height // 8
    my_row = lax.axis_index("row")
    my_col = lax.axis_index("col")

    def exists(dr, dc):
        answer = None
        for shift, place, count in ((dr, my_row, rows), (dc, my_col, cols)):
            if shift == 0:
                continue
            test = place + shift < count if shift > 0 else place + shift >= 0
            answer = test if answer is None else jnp.logical_and(answer, test)
        return answer

    lane = lax.broadcasted_iota(jnp.int32, (8, width), 1)

    exchanges = [(state_e, state_cs, state_cr)] + [
        (field_e.at[n], field_cs.at[n], field_cr.at[n]) for n in range(3)
    ]
    loads = [
        pltpu.make_async_copy(source, target, input_sem.at[n])
        for n, (source, target) in enumerate(
            (
                (counts_hbm, counts_ref),
                (vel_hbm, vel_ref),
                (off_hbm, off_ref),
                (mass_hbm, mass_ref),
                (low_hbm, low_ref),
                (high_hbm, high_ref),
            )
        )
    ]
    for load in loads:
        load.start()

    barrier = pltpu.get_barrier_semaphore()
    for dr, dc in DIRECTIONS:

        @pl.when(exists(dr, dc))
        def _(dr=dr, dc=dc):
            pl.semaphore_signal(
                barrier, inc=1, device_id=(my_row + dr, my_col + dc), device_id_type=MESH
            )

    for e_ref, _, cr_ref in exchanges:
        planes = e_ref.shape[0]
        for dr, begin in ((-1, 0), (1, height + 8)):

            @pl.when(jnp.logical_not(exists(dr, 0)))
            def _(e_ref=e_ref, begin=begin, planes=planes):
                e_ref[:, begin : begin + 8, :] = jnp.zeros((planes, 8, width), jnp.float32)

        for side, dc in ((0, -1), (1, 1)):
            for dr, begin, size in ((-1, 0, 8), (0, 8, height), (1, height + 8, 8)):

                @pl.when(jnp.logical_not(exists(dr, dc)))
                def _(cr_ref=cr_ref, side=side, begin=begin, size=size):
                    cr_ref[side, begin : begin + size, :] = jnp.zeros((size, width), jnp.float32)

    for load in loads:
        load.wait()

    for slot in range(slots):
        occupied = jnp.where(counts_ref[...] > slot, 1.0, 0.0).astype(jnp.float32)
        inner = slice(8, 8 + height)
        for axis in range(2):
            speed = vel_ref[axis, slot]
            state_e[axis * slots + slot, inner, :] = 0.5 * (off_ref[axis, slot] + TIME_STEP * speed)
            state_e[(2 + axis) * slots + slot, inner, :] = speed
        state_e[4 * slots + slot, inner, :] = SLOPE_NORM * (mass_ref[slot] * occupied)

    def pack(e_ref, cs_ref):
        planes = e_ref.shape[0]

        def tile(number, carry):
            begin = number * 8 if isinstance(number, int) else pl.multiple_of(number * 8, 8)
            left = jnp.zeros((8, width), jnp.float32)
            right = jnp.zeros((8, width), jnp.float32)
            for plane in range(planes):
                value = e_ref[plane, pl.ds(begin + 8, 8), :]
                if plane:
                    value = pltpu.roll(value, 4 * plane, 1)
                at = 4 * plane
                left = jnp.where((lane == at) | (lane == at + 1), value, left)
                low = (at - 2) % width
                right = jnp.where((lane == low) | (lane == low + 1), value, right)
            cs_ref[0, pl.ds(begin, 8), :] = left
            cs_ref[1, pl.ds(begin, 8), :] = right
            return carry

        if planes > slots:
            lax.fori_loop(0, steps, tile, 0)
        else:
            for number in range(steps):
                tile(number, 0)

    def copy(number, way):
        e_ref, cs_ref, cr_ref = exchanges[number]
        dr, dc = DIRECTIONS[way]
        if dc == 0:
            if dr > 0:
                source, target = e_ref.at[:, height : height + 8, :], e_ref.at[:, 0:8, :]
            else:
                source = e_ref.at[:, 8:16, :]
                target = e_ref.at[:, height + 8 : height + 16, :]
        else:
            mine, theirs = (1, 0) if dc > 0 else (0, 1)
            if dr == 0:
                source, target = cs_ref.at[mine], cr_ref.at[theirs, 8 : 8 + height, :]
            elif dr > 0:
                source = cs_ref.at[mine, height - 8 : height, :]
                target = cr_ref.at[theirs, 0:8, :]
            else:
                source = cs_ref.at[mine, 0:8, :]
                target = cr_ref.at[theirs, height + 8 : height + 16, :]
        return pltpu.make_async_remote_copy(
            src_ref=source,
            dst_ref=target,
            send_sem=send_sem.at[number, way],
            recv_sem=recv_sem.at[number, way],
            device_id=(my_row + dr, my_col + dc),
            device_id_type=MESH,
        )

    def send(number):
        for way in (4, 5, 6, 7, 2, 3, 0, 1):

            @pl.when(exists(*DIRECTIONS[way]))
            def _(way=way):
                copy(number, way).start()

    def receive(number, ways):
        for way in ways:
            dr, dc = DIRECTIONS[way]

            @pl.when(exists(-dr, -dc))
            def _(way=way):
                copy(number, way).wait_recv()

    def drain(number):
        for way in range(8):

            @pl.when(exists(*DIRECTIONS[way]))
            def _(way=way):
                copy(number, way).wait_send()

    def spread(number, near_ref, k, shifts):
        e_ref, _, cr_ref = exchanges[number]
        planes = e_ref.shape[0]
        lines = pl.ds(6 + k, 8, stride=8)
        if shifts != (0,):
            rim = cr_ref[0, lines, :] + cr_ref[1, lines, :]
        for plane in range(planes):
            value = e_ref[plane, lines, :]
            along = planes > slots and slots <= plane < 2 * slots
            for shift in shifts:
                moved = value
                if shift:
                    rolled = pltpu.roll(value, -shift % width, 1)
                    edge = pltpu.roll(rim, (-4 * plane - shift) % width, 1) if 4 * plane + shift else rim
                    inner = lane < width - shift if shift > 0 else lane >= -shift
                    moved = jnp.where(inner, rolled, edge)
                if along and shift:
                    moved = moved + 0.5 * shift
                near_ref[shift + 2, plane, k] = moved

    def spread_lines(number, near_ref, begins, shifts):
        first, gap, count = begins

        def lines(index, carry):
            for k in range(2):
                spread(number, near_ref, first + index * gap + k, shifts)
            return carry

        if near_ref.shape[1] > slots:
            lax.fori_loop(0, count, lines, 0)
        else:
            for index in range(count):
                lines(index, 0)

    inside = (2, 2, steps // 2)
    outside = (0, steps + 2, 2)
    beside = (-2, -1, 1, 2)
    everywhere = (-2, -1, 0, 1, 2)

    def inner_lines(work):
        def body(t, carry):
            work(t)
            return carry

        lax.fori_loop(2, steps - 2, body, 0)

    def outer_lines(work):
        def body(index, carry):
            work(index + (index // 2) * (steps - 4))
            return carry

        lax.fori_loop(0, 4, body, 0)

    pack(state_e, state_cs)
    tall = 1 + jnp.where(my_row > 0, 1, 0) + jnp.where(my_row + 1 < rows, 1, 0)
    wide = 1 + jnp.where(my_col > 0, 1, 0) + jnp.where(my_col + 1 < cols, 1, 0)
    pl.semaphore_wait(barrier, tall * wide - 1)

    send(0)
    spread_lines(0, near_s, inside, (0,))

    full = (8, width)
    low = jnp.broadcast_to(low_ref[0], full)
    high = jnp.broadcast_to(high_ref[0], full)
    middle = 0.5 * (high + low)
    radius = 0.5 * (high - low)
    quotient = middle / radius
    factor_zero = 1.0 / quotient
    factor_one = 1.0 / (2.0 * quotient - factor_zero)
    factor_two = 1.0 / (2.0 * quotient - factor_one)
    over_middle = 1.0 / middle
    keep_one = factor_one * factor_zero
    keep_two = factor_two * factor_one
    gain_one = 2.0 * factor_one / radius
    gain_two = 2.0 * factor_two / radius

    def own_state(field, t):
        return near_s[2, field * slots : (field + 1) * slots, t + 2]

    def put_field(number, t, value):
        for slot in range(slots):
            field_e[number, slot, pl.ds(8 + t, 8, stride=8), :] = value[slot]

    zero = jnp.zeros((slots, 8, width), jnp.float32)

    def flow(t, shifts, sums):
        own_x = own_state(0, t)
        own_y = own_state(1, t)
        own_vx = own_state(2, t)
        own_vy = own_state(3, t)

        def along(e, sums):
            dens, inflow, slope_sum = sums
            base_x = own_x - 0.5 * jnp.asarray(e - 2, jnp.float32)
            for f in shifts:
                for b in range(slots):
                    dx = near_s[f, b, t + e][None] - base_x
                    dy = near_s[f, slots + b, t + e][None] - own_y
                    square = dx * dx + dy * dy
                    q = square * lax.rsqrt(jnp.maximum(square, TINY))
                    u = jnp.maximum(1.0 - q, 0.0)
                    slope = near_s[f, 4 * slots + b, t + e][None] * (u * u * u)
                    slopes_ref[t * 5 + e, f, b] = slope
                    dens = dens + slope * (u * (1.25 - u))
                    slope_sum = slope_sum + slope
                    dvx = near_s[f, 2 * slots + b, t + e][None] - own_vx
                    dvy = near_s[f, 3 * slots + b, t + e][None] - own_vy
                    inflow = inflow + slope * (dvx * dx + dvy * dy)
            return dens, inflow, slope_sum

        if len(shifts) == 1:
            for e in range(5):
                sums = along(e, sums)
            return sums
        return lax.fori_loop(0, 5, along, sums)

    def finish(t, sums):
        dens, inflow, slope_sum = sums
        density = BACKGROUND + dens * (4.0 * KERNEL_NORM / SLOPE_NORM)
        inverse = 1.0 / density
        source = inflow * inverse * (-2.0 / TIME_STEP)
        first = source * over_middle[None]
        own_ref[0, t] = inverse
        own_ref[1, t] = DIAGONAL_SHIFT + 2.0 * inverse * slope_sum
        own_ref[2, t] = source
        own_ref[3, t] = first
        put_field(0, t, first)

    def flow_start(t):
        for n, value in enumerate(flow(t, (2,), (zero, zero, zero))):
            sums_ref[n, t] = value

    def flow_beside(t):
        sums = tuple(sums_ref[n, t] for n in range(3))
        finish(t, flow(t, (0, 1, 3, 4), sums))

    def flow_whole(t):
        finish(t, flow(t, (0, 1, 2, 3, 4), (zero, zero, zero)))

    inner_lines(flow_start)
    receive(0, (2, 3))
    spread_lines(0, near_s, inside, beside)
    inner_lines(flow_beside)
    receive(0, (0, 1, 4, 5, 6, 7))
    spread_lines(0, near_s, outside, everywhere)
    outer_lines(flow_whole)

    def gather(t, low_e, high_e, sums):
        def along(e, totals):
            totals = list(totals)
            for f in range(5):
                for b in range(slots):
                    near = near_p[f, b, t + e][None]
                    totals[b % 2] = totals[b % 2] + slopes_ref[t * 5 + e, f, b] * near
            return tuple(totals)

        return lax.fori_loop(low_e, high_e, along, sums)

    def push_part(t, low_e, high_e, sums):
        solved = own_ref[3, t]

        def along(e, sums):
            push_x, push_y, push = sums
            shift = 0.5 * jnp.asarray(e - 2, jnp.float32)
            for f in range(5):
                for b in range(slots):
                    part = slopes_ref[t * 5 + e, f, b] * (near_p[f, b, t + e][None] - solved)
                    push = push + part
                    push_x = push_x + part * (near_s[f, b, t + e] + shift)[None]
                    push_y = push_y + part * near_s[f, slots + b, t + e][None]
            return push_x, push_y, push

        return lax.fori_loop(low_e, high_e, along, sums)

    def sweep(number, count, part, finish):
        start = (zero,) * count
        outer = (0, 1, steps - 2, steps - 1)
        pack(field_e.at[number], field_cs.at[number])
        send(number + 1)
        spread_lines(number + 1, near_p, inside, (0,))
        receive(number + 1, (2, 3))
        spread_lines(number + 1, near_p, inside, beside)
        inner_lines(lambda t: finish(t, part(t, 0, 5, start)))
        for t in outer:
            sums = part(t, max(0, 2 - t), min(5, steps + 2 - t), start)
            for n, value in enumerate(sums):
                sums_ref[n, t] = value
        receive(number + 1, (0, 1, 4, 5, 6, 7))
        spread_lines(number + 1, near_p, outside, everywhere)
        for t in outer:
            sums = tuple(sums_ref[n, t] for n in range(count))
            if t < 2:
                sums = part(t, 0, 2 - t, sums)
            else:
                sums = part(t, steps + 2 - t, 5, sums)
            finish(t, sums)

    def second_step(t, sums):
        field = own_ref[3, t]
        residual = own_ref[2, t] - (own_ref[1, t] * field - 2.0 * own_ref[0, t] * (sums[0] + sums[1]))
        second = keep_one[None] * field + gain_one[None] * residual
        own_ref[2, t] = residual
        own_ref[4, t] = second
        put_field(1, t, second)

    def third_step(t, sums):
        field = own_ref[4, t]
        residual = own_ref[2, t] - (own_ref[1, t] * field - 2.0 * own_ref[0, t] * (sums[0] + sums[1]))
        third = keep_two[None] * field + gain_two[None] * residual
        solved = own_ref[3, t] + field + third
        own_ref[3, t] = solved
        put_field(2, t, solved)

    def kick(t, sums):
        own_x = own_state(0, t)
        own_y = own_state(1, t)
        solved = own_ref[3, t]
        push_x, push_y, push = sums
        scale = own_ref[0, t] * (2.0 * TIME_STEP)
        new_x = own_state(2, t) - scale * (push_x - own_x * push)
        new_y = own_state(3, t) - scale * (push_y - own_y * push)
        live = counts_ref[pl.ds(t, 8, stride=8), :]
        for slot in range(slots):
            occupied = jnp.where(live > slot, 1.0, 0.0).astype(jnp.float32)
            nv_ref[0, slot, pl.ds(t, 8, stride=8), :] = occupied * new_x[slot]
            nv_ref[1, slot, pl.ds(t, 8, stride=8), :] = occupied * new_y[slot]
            press_ref[slot, pl.ds(t, 8, stride=8), :] = occupied * solved[slot]

    sweep(0, 2, gather, second_step)
    sweep(1, 2, gather, third_step)
    sweep(2, 3, push_part, kick)
    for number in range(4):
        drain(number)


def on_device(rows, cols, offsets, velocity, mass, counts, spectrum_low, spectrum_high):
    slots, height, width = mass.shape
    assert height % 16 == 0 and height >= 48 and width % 128 == 0
    steps = height // 8
    planes = 5 * slots
    results = 4 * (velocity.size + mass.size)
    vmem = pl.BlockSpec(memory_space=pltpu.VMEM)
    hbm = pl.BlockSpec(memory_space=pltpu.HBM)

    def room(*shape):
        return pltpu.VMEM(shape, jnp.float32)

    return pl.pallas_call(
        functools.partial(kernel, rows, cols),
        out_shape=(
            pltpu.VMEM(velocity.shape, jnp.float32),
            pltpu.VMEM(mass.shape, jnp.float32),
        ),
        in_specs=[hbm] * 6,
        out_specs=(vmem, vmem),
        scratch_shapes=[
            room(*offsets.shape),
            room(*velocity.shape),
            room(*mass.shape),
            pltpu.VMEM(counts.shape, jnp.int32),
            pltpu.SMEM(spectrum_low.shape, jnp.float32),
            pltpu.SMEM(spectrum_high.shape, jnp.float32),
            room(3, steps, slots, 8, width),
            pltpu.SemaphoreType.DMA((6,)),
            room(planes, height + 16, width),
            room(2, height, width),
            room(2, height + 16, width),
            room(3, slots, height + 16, width),
            room(3, 2, height, width),
            room(3, 2, height + 16, width),
            room(5, planes, steps + 4, 8, width),
            room(5, slots, steps + 4, 8, width),
            room(steps * 5, 5, slots, slots, 8, width),
            room(5, steps, slots, 8, width),
            pltpu.SemaphoreType.DMA((4, 8)),
            pltpu.SemaphoreType.DMA((4, 8)),
        ],
        compiler_params=pltpu.CompilerParams(
            collective_id=0, has_side_effects=True, vmem_limit_bytes=VMEM_BYTES - results - SPARE
        ),
        name="sph_step",
    )(offsets, velocity, mass, counts, spectrum_low, spectrum_high)


def solution(mesh):
    placed = (
        P(None, None, "row", "col"),
        P(None, None, "row", "col"),
        P(None, "row", "col"),
        P("row", "col"),
        P(),
        P(),
    )
    return jax.shard_map(
        functools.partial(on_device, mesh.shape["row"], mesh.shape["col"]),
        mesh=mesh,
        in_specs=placed,
        out_specs=(P(None, None, "row", "col"), P(None, "row", "col")),
        check_vma=False,
    )
```

```python
import functools
import math

import jax
import jax.numpy as jnp
from jax import lax
from jax.experimental import pallas as pl
from jax.experimental.pallas import tpu as pltpu
from jax.sharding import PartitionSpec as P

TIME_STEP = 0.1
KERNEL_NORM = 7.0 / (4.0 * math.pi)
SLOPE_NORM = 20.0 * KERNEL_NORM / 4.0
BACKGROUND = 0.5 * KERNEL_NORM
DIAGONAL_SHIFT = 1.0
REACH = 4.0 / 3.0
CELL = REACH / 2.0
VMEM_BYTES = 67_043_328
SPARE = 8192
MESH = pl.DeviceIdType.MESH
DIRECTIONS = ((1, 0), (-1, 0), (0, 1), (0, -1), (1, 1), (-1, 1), (1, -1), (-1, -1))


def kernel(
    rows,
    cols,
    off_hbm,
    vel_hbm,
    mass_hbm,
    counts_hbm,
    low_hbm,
    high_hbm,
    nv_ref,
    press_ref,
    off_ref,
    vel_ref,
    mass_ref,
    counts_ref,
    low_ref,
    high_ref,
    input_sem,
    tile_ref,
    above_ref,
    edge_ref,
    beside_ref,
    bend_ref,
    corner_ref,
    near_ref,
    around_ref,
    slopes_ref,
    moment_ref,
    own_ref,
    send_sem,
    recv_sem,
):
    slots, height, width = mass_hbm.shape
    steps = height // 8
    span = width // steps
    strip, corners, tops = steps, steps + 1, steps + 2
    planes = 5 * slots
    batch = width // span
    my_row = lax.axis_index("row")
    my_col = lax.axis_index("col")

    def exists(dr, dc):
        answer = None
        for shift, place, length in ((dr, my_row, rows), (dc, my_col, cols)):
            if shift == 0:
                continue
            test = place + shift < length if shift > 0 else place + shift >= 0
            answer = test if answer is None else jnp.logical_and(answer, test)
        return answer

    lane = lax.broadcasted_iota(jnp.int32, (8, width), 1)
    line = lax.broadcasted_iota(jnp.int32, (8, width), 0)
    place = lane % span
    block = ((lane + span // 2) % width) // span
    left_half = place < span // 2
    inverse_at, diagonal_at, residual_at, moment_at, sum_at, step_at = 0, 1, 2, 3, 5, 6

    loads = [
        pltpu.make_async_copy(source, target, input_sem.at[n])
        for n, (source, target) in enumerate(
            (
                (counts_hbm, counts_ref),
                (vel_hbm, vel_ref),
                (off_hbm, off_ref),
                (mass_hbm, mass_ref),
                (low_hbm, low_ref),
                (high_hbm, high_ref),
            )
        )
    ]
    for load in loads:
        load.start()

    barrier = pltpu.get_barrier_semaphore()
    for dr, dc in DIRECTIONS:

        @pl.when(exists(dr, dc))
        def _(dr=dr, dc=dc):
            pl.semaphore_signal(
                barrier, inc=1, device_id=(my_row + dr, my_col + dc), device_id_type=MESH
            )

    for side, dr in ((0, -1), (1, 1)):

        @pl.when(jnp.logical_not(exists(dr, 0)))
        def _(side=side):
            above_ref[side] = jnp.zeros(above_ref.shape[1:], jnp.float32)

    for side, dc in ((0, -1), (1, 1)):

        @pl.when(jnp.logical_not(exists(0, dc)))
        def _(side=side):
            beside_ref[side] = jnp.zeros(beside_ref.shape[1:], jnp.float32)

        for level, dr in ((0, -1), (1, 1)):

            @pl.when(jnp.logical_not(exists(dr, dc)))
            def _(side=side, level=level):
                corner_ref[side, level] = jnp.zeros(corner_ref.shape[2:], jnp.float32)

    for load in loads:
        load.wait()

    def particles(window, put):
        live = counts_ref[window, :]
        for slot in range(slots):
            occupied = jnp.where(live > slot, 1.0, 0.0).astype(jnp.float32)
            for axis in range(2):
                speed = vel_ref[axis, slot, window, :]
                place = off_ref[axis, slot, window, :] + TIME_STEP * speed
                put(axis * slots + slot, CELL * place)
                put((2 + axis) * slots + slot, speed)
            weight = mass_ref[slot, window, :] * occupied
            put(4 * slots + slot, (SLOPE_NORM / REACH**3) * weight)

    def own_tile(s, carry):
        window = pl.ds(pl.multiple_of(8 * s, 8), 8)

        def put_tile(plane, value):
            tile_ref[plane, window, :] = value

        particles(window, put_tile)
        return carry

    lax.fori_loop(0, steps, own_tile, 0)

    def lane_roll(value, shift):
        shift = shift % width
        return pltpu.roll(value, shift, 1) if shift else value

    def under(value, shift):
        return pltpu.roll(value, shift % 8, 0)

    def edges(plane):
        packed = tile_ref[plane, 0:8, :]
        for s in range(1, steps):
            moved = lane_roll(tile_ref[plane, 8 * s : 8 * s + 8, :], span * s)
            packed = jnp.where(block == s, moved, packed)
        return packed

    def each_plane(work):
        def body(index, carry):
            for n in range(slots):
                work(index * slots + n)
            return carry

        lax.fori_loop(0, planes // slots, body, 0)

    def pack(plane):
        edge_ref[plane] = edges(plane)

    each_plane(pack)

    for level, home in ((0, steps - 1), (1, 0)):
        for g in range(bend_ref.shape[1]):
            packed = None
            for n in range(min(batch, planes - g * batch)):
                moved = lane_roll(edge_ref[g * batch + n], span * (n - home))
                packed = moved if packed is None else jnp.where(block == n, moved, packed)
            bend_ref[level, g] = packed

    def copy(way):
        dr, dc = DIRECTIONS[way]
        theirs = 0 if dc > 0 else 1
        if dc == 0 and dr > 0:
            source, target = tile_ref.at[:, height - 8 : height, :], above_ref.at[0]
        elif dc == 0:
            source, target = tile_ref.at[:, 0:8, :], above_ref.at[1]
        elif dr == 0:
            source, target = edge_ref, beside_ref.at[theirs]
        else:
            level = 0 if dr > 0 else 1
            source, target = bend_ref.at[level], corner_ref.at[theirs, level]
        return pltpu.make_async_remote_copy(
            src_ref=source,
            dst_ref=target,
            send_sem=send_sem.at[way],
            recv_sem=recv_sem.at[way],
            device_id=(my_row + dr, my_col + dc),
            device_id_type=MESH,
        )

    tall = 1 + jnp.where(my_row > 0, 1, 0) + jnp.where(my_row + 1 < rows, 1, 0)
    wide = 1 + jnp.where(my_col > 0, 1, 0) + jnp.where(my_col + 1 < cols, 1, 0)
    pl.semaphore_wait(barrier, tall * wide - 1)
    for way in (4, 5, 6, 7, 2, 3, 0, 1):

        @pl.when(exists(*DIRECTIONS[way]))
        def _(way=way):
            copy(way).start()

    def own_line(plane):
        for t in range(steps):
            value = tile_ref[plane, pl.ds(t, 8, stride=8), :]
            for f in range(5):
                near_ref[f, plane, t + 2] = lane_roll(value, 2 - f)

    each_plane(own_line)

    def near_line(t):
        return lambda e, f, plane: near_ref[f, plane, t + e]

    def near_around(n):
        return lambda e, f, plane: around_ref[n, e, f, plane]

    def own(near, first):
        return jnp.stack([near(2, 2, first * slots + slot) for slot in range(slots)])

    zero = jnp.zeros((slots, 8, width), jnp.float32)
    start = (zero,) * 5

    def flow(x, near, low_e, high_e, sums, moments):
        own_x = own(near, 0)
        own_y = own(near, 1)

        def along(e, sums):
            slope_sum, dens, flux, sum_x, sum_y = sums
            base_x = own_x - CELL * jnp.asarray(e - 2, jnp.float32)
            for f in range(5):
                base_y = own_y - CELL * (f - 2) if f != 2 else own_y
                for b in range(slots):
                    dx = near(e, f, b)[None] - base_x
                    dy = near(e, f, slots + b)[None] - base_y
                    square = dx * dx + dy * dy
                    inverse = lax.rsqrt(square)
                    dist = lax.rsqrt(inverse * inverse)
                    u = jnp.maximum(REACH - dist, 0.0)
                    slope = (u * u) * (near(e, f, 4 * slots + b)[None] * u)
                    slopes_ref[x * 5 + e, f, b] = slope
                    slope_sum = slope_sum + slope
                    dens = dens + slope * (dist - square)
                    moment_x = slope * dx
                    moment_y = slope * dy
                    if moments:
                        moment_ref[0, x * 5 + e, f, b] = moment_x
                        moment_ref[1, x * 5 + e, f, b] = moment_y
                    flux = flux + moment_x * near(e, f, 2 * slots + b)[None]
                    flux = flux + moment_y * near(e, f, 3 * slots + b)[None]
                    sum_x = sum_x + moment_x
                    sum_y = sum_y + moment_y
            return slope_sum, dens, flux, sum_x, sum_y

        return lax.fori_loop(low_e, high_e, along, sums)

    def save(x, sums):
        for n, value in enumerate(sums):
            own_ref[n, x] = value

    def saved(x):
        return tuple(own_ref[n, x] for n in range(5))

    def each(first, last, work):
        def body(x, carry):
            work(x)
            return carry

        lax.fori_loop(first, last, body, 0)

    def flow_inner(t):
        low_e = jnp.maximum(0, 2 - t)
        high_e = jnp.minimum(5, steps + 2 - t)
        save(t, flow(t, near_line(t), low_e, high_e, start, True))

    def flow_outer(index):
        t = index + (index // 2) * (steps - 4)
        low_e = jnp.where(t < 2, 0, steps + 2 - t)
        high_e = jnp.where(t < 2, 2 - t, 5)
        save(t, flow(t, near_line(t), low_e, high_e, saved(t), True))

    each(0, steps, flow_inner)

    for way in range(8):
        dr, dc = DIRECTIONS[way]

        @pl.when(exists(-dr, -dc))
        def _(way=way):
            copy(way).wait_recv()

    def ring(plane, top, bottom):
        for f in range(5):
            above, below = lane_roll(top, 2 - f), lane_roll(bottom, 2 - f)
            first, second = near_ref[f, plane, 2], near_ref[f, plane, 3]
            before, last = near_ref[f, plane, steps], near_ref[f, plane, steps + 1]
            near_ref[f, plane, 0] = jnp.where(line == 0, under(above, 2), under(before, 1))
            near_ref[f, plane, 1] = jnp.where(line == 0, under(above, 1), under(last, 1))
            near_ref[f, plane, steps + 2] = jnp.where(line == 7, under(below, 7), under(first, 7))
            near_ref[f, plane, steps + 3] = jnp.where(line == 7, under(below, 6), under(second, 7))
            around_ref[2, 0, f, plane] = under(above, 2)
            around_ref[2, 1, f, plane] = under(above, 1)
            around_ref[2, 2, f, plane] = above
            around_ref[2, 3, f, plane] = jnp.where(line == 7, under(first, 7), under(above, 7))
            beyond = jnp.where(line == 7, under(second, 7), under(above, 6))
            around_ref[2, 4, f, plane] = jnp.where(line == 6, under(first, 6), beyond)
            beyond = jnp.where(line == 1, under(last, 2), under(below, 2))
            around_ref[3, 0, f, plane] = jnp.where(line == 0, under(before, 1), beyond)
            around_ref[3, 1, f, plane] = jnp.where(line == 0, under(last, 1), under(below, 1))
            around_ref[3, 2, f, plane] = below
            around_ref[3, 3, f, plane] = under(below, 7)
            around_ref[3, 4, f, plane] = under(below, 6)

    def widen(plane, inner, outer):
        for f in range(5):
            mine = (lane + (span + 2 - f)) % span < span // 2
            here = lane_roll(jnp.where(mine, *inner), 2 - f)
            bend = lane_roll(jnp.where(mine, *outer), 2 - f)
            after = jnp.where(lane >= width - span, bend, lane_roll(here, -span))
            ahead = jnp.where(lane < span, bend, lane_roll(here, span))
            for n, value, up, down in ((0, here, after, ahead), (1, bend, here, here)):
                around_ref[n, 0, f, plane] = under(jnp.where(line >= 6, down, value), 2)
                around_ref[n, 1, f, plane] = under(jnp.where(line >= 7, down, value), 1)
                around_ref[n, 2, f, plane] = value
                around_ref[n, 3, f, plane] = under(jnp.where(line < 1, up, value), 7)
                around_ref[n, 4, f, plane] = under(jnp.where(line < 2, up, value), 6)

    def fold(top, bottom):
        return jnp.where(block == 0, top, lane_roll(bottom, span * (steps - 1)))

    def arrive(plane, g, n):
        top, bottom = above_ref[0, plane], above_ref[1, plane]
        ring(plane, top, bottom)

        def strips(mine, theirs):
            left = lane_roll(jnp.where(left_half, mine, theirs), 6)
            right = lane_roll(jnp.where(left_half, theirs, mine), 10)
            return left, right

        inner = jnp.where(left_half, beside_ref[1, plane], beside_ref[0, plane])
        ends = [jnp.where(left_half, corner_ref[1, level, g], corner_ref[0, level, g]) for level in (0, 1)]
        outer = fold(lane_roll(ends[0], -span * n), lane_roll(ends[1], -span * n))
        widen(plane, strips(edge_ref[plane], inner), strips(fold(top, bottom), outer))

    def arrive_some(index, carry):
        g = index // 2
        for half in range(2):

            @pl.when(index % 2 == half)
            def _(half=half):
                for n in range(slots):
                    arrive(index * slots + n, g, half * slots + n)

        return carry

    lax.fori_loop(0, planes // slots, arrive_some, 0)

    each(0, 4, flow_outer)
    save(strip, flow(strip, near_around(0), 0, 5, start, True))
    each(1, 4, lambda n: save(steps + n, flow(steps + n, near_around(n), 0, 5, start, False)))

    full = (8, width)
    low = jnp.broadcast_to(low_ref[0], full)
    high = jnp.broadcast_to(high_ref[0], full)
    middle = 0.5 * (high + low)
    radius = 0.5 * (high - low)
    quotient = middle / radius
    factor_zero = 1.0 / quotient
    factor_one = 1.0 / (2.0 * quotient - factor_zero)
    factor_two = 1.0 / (2.0 * quotient - factor_one)
    over_middle = 1.0 / middle
    keep_one = factor_one * factor_zero
    keep_two = factor_two * factor_one
    gain_one = 2.0 * factor_one / radius
    gain_two = 2.0 * factor_two / radius

    def everyone(work):
        each(0, steps, lambda t: work(t, near_line(t)))
        each(0, 4, lambda n: work(steps + n, near_around(n)))

    def first_step(x, near):
        slope_sum, dens, flux, sum_x, sum_y = saved(x)
        density = BACKGROUND + (KERNEL_NORM / SLOPE_NORM) * (slope_sum + (4.0 / REACH**2) * dens)
        inverse = 1.0 / density
        inflow = flux - own(near, 2) * sum_x - own(near, 3) * sum_y
        source = inflow * inverse * (-1.0 / (CELL * TIME_STEP))
        own_ref[inverse_at, x] = inverse
        own_ref[diagonal_at, x] = DIAGONAL_SHIFT + 2.0 * inverse * slope_sum
        own_ref[residual_at, x] = source
        own_ref[sum_at, x] = source * over_middle[None]

    def turn(value):
        return jnp.where(left_half, lane_roll(value, -2), lane_roll(value, 2))

    def mend(value, turned, s):
        outermost = (lane < 2) | (lane >= width - 2)
        return jnp.where(outermost, lane_roll(turned, -span * s - span // 2), value)

    def refresh(at):
        for slot in range(slots):
            for t in range(steps):
                tile_ref[slot, pl.ds(t, 8, stride=8), :] = own_ref[at, t, slot]
            inner, outer = own_ref[at, strip, slot], own_ref[at, corners, slot]
            turned = turn(inner)
            for s in range(steps):
                window = slice(8 * s, 8 * s + 8)
                tile_ref[slot, window, :] = mend(tile_ref[slot, window, :], turned, s)
            turned = turn(outer)
            top = mend(own_ref[at, tops, slot], turned, 0)
            bottom = mend(own_ref[at, tops + 1, slot], turned, steps - 1)
            own_line(slot)
            ring(slot, top, bottom)

            def strips(value, mine):
                left = jnp.where(left_half, value, lane_roll(mine, 6))
                right = jnp.where(left_half, lane_roll(mine, 10), value)
                return left, right

            widen(slot, strips(inner, edges(slot)), strips(outer, fold(top, bottom)))

    def gather(x, near):
        def along(e, totals):
            totals = list(totals)
            for f in range(5):
                for b in range(slots):
                    value = near(e, f, b)[None]
                    totals[b % 2] = totals[b % 2] + slopes_ref[x * 5 + e, f, b] * value
            return tuple(totals)

        even, odd = lax.fori_loop(0, 5, along, (zero, zero))
        return even + odd

    def improve(x, near, here):
        total = gather(x, near)
        change = own_ref[diagonal_at, x] * here - 2.0 * own_ref[inverse_at, x] * total
        residual = own_ref[residual_at, x] - change
        own_ref[residual_at, x] = residual
        return residual

    def second_step(x, near):
        here = own_ref[sum_at, x]
        own_ref[step_at, x] = keep_one[None] * here + gain_one[None] * improve(x, near, here)

    def third_step(x, near):
        here = own_ref[step_at, x]
        third = keep_two[None] * here + gain_two[None] * improve(x, near, here)
        own_ref[sum_at, x] = own_ref[sum_at, x] + here + third

    def push(x, near):
        def along(e, totals):
            push_x, push_y = totals
            for f in range(5):
                for b in range(slots):
                    value = near(e, f, b)[None]
                    push_x = push_x + moment_ref[0, x * 5 + e, f, b] * value
                    push_y = push_y + moment_ref[1, x * 5 + e, f, b] * value
            return push_x, push_y

        pushes = lax.fori_loop(0, 5, along, (zero, zero))
        solved = own_ref[sum_at, x]
        scale = own_ref[inverse_at, x] * (TIME_STEP / CELL)
        return [
            own(near, 2 + axis) - scale * (pushes[axis] - solved * own_ref[moment_at + axis, x])
            for axis in range(2)
        ]

    def kick_line(t):
        for axis, value in enumerate(push(t, near_line(t))):
            for slot in range(slots):
                nv_ref[axis, slot, pl.ds(t, 8, stride=8), :] = value[slot]

    def kick_ends():
        turned = [[turn(value[slot]) for slot in range(slots)] for value in push(strip, near_around(0))]
        for s in range(steps):
            window = slice(8 * s, 8 * s + 8)
            live = counts_ref[window, :]
            for slot in range(slots):
                occupied = jnp.where(live > slot, 1.0, 0.0).astype(jnp.float32)
                for axis in range(2):
                    value = mend(nv_ref[axis, slot, window, :], turned[axis][slot], s)
                    nv_ref[axis, slot, window, :] = occupied * value
                press_ref[slot, window, :] = occupied * tile_ref[slot, window, :]

    for way in range(8):

        @pl.when(exists(*DIRECTIONS[way]))
        def _(way=way):
            copy(way).wait_send()

    everyone(first_step)
    refresh(sum_at)
    everyone(second_step)
    refresh(step_at)
    everyone(third_step)
    refresh(sum_at)
    each(0, steps, kick_line)
    kick_ends()

def on_device(rows, cols, offsets, velocity, mass, counts, spectrum_low, spectrum_high):
    slots, height, width = mass.shape
    steps = height // 8
    span = width // steps
    assert height % 8 == 0 and steps == 8 and width % 128 == 0 and span == 16
    planes = 5 * slots
    bends = -(-planes * span // width)
    count = steps + 4
    results = 4 * (velocity.size + mass.size)
    vmem = pl.BlockSpec(memory_space=pltpu.VMEM)
    hbm = pl.BlockSpec(memory_space=pltpu.HBM)

    def room(*shape):
        return pltpu.VMEM(shape, jnp.float32)

    return pl.pallas_call(
        functools.partial(kernel, rows, cols),
        out_shape=(
            pltpu.VMEM(velocity.shape, jnp.float32),
            pltpu.VMEM(mass.shape, jnp.float32),
        ),
        in_specs=[hbm] * 6,
        out_specs=(vmem, vmem),
        scratch_shapes=[
            room(*offsets.shape),
            room(*velocity.shape),
            room(*mass.shape),
            pltpu.VMEM(counts.shape, jnp.int32),
            pltpu.SMEM(spectrum_low.shape, jnp.float32),
            pltpu.SMEM(spectrum_high.shape, jnp.float32),
            pltpu.SemaphoreType.DMA((6,)),
            room(planes, height, width),
            room(2, planes, 8, width),
            room(planes, 8, width),
            room(2, planes, 8, width),
            room(2, bends, 8, width),
            room(2, 2, bends, 8, width),
            room(5, planes, steps + 4, 8, width),
            room(4, 5, 5, planes, 8, width),
            room(count * 5, 5, slots, slots, 8, width),
            room(2, (steps + 1) * 5, 5, slots, slots, 8, width),
            room(7, count, slots, 8, width),
            pltpu.SemaphoreType.DMA((8,)),
            pltpu.SemaphoreType.DMA((8,)),
        ],
        compiler_params=pltpu.CompilerParams(
            collective_id=0,
            has_side_effects=True,
            vmem_limit_bytes=VMEM_BYTES - results - SPARE,
        ),
        name="sph_step",
    )(offsets, velocity, mass, counts, spectrum_low, spectrum_high)


def solution(mesh):
    placed = (
        P(None, None, "row", "col"),
        P(None, None, "row", "col"),
        P(None, "row", "col"),
        P("row", "col"),
        P(),
        P(),
    )
    return jax.shard_map(
        functools.partial(on_device, mesh.shape["row"], mesh.shape["col"]),
        mesh=mesh,
        in_specs=placed,
        out_specs=(P(None, None, "row", "col"), P(None, "row", "col")),
        check_vma=False,
    )
```

```python
import functools
import math

import jax
import jax.numpy as jnp
from jax import lax
from jax.experimental import pallas as pl
from jax.experimental.pallas import tpu as pltpu
from jax.sharding import PartitionSpec as P

TIME_STEP = 0.1
KERNEL_NORM = 7.0 / (4.0 * math.pi)
SLOPE_NORM = 20.0 * KERNEL_NORM / 4.0
BACKGROUND = 0.5 * KERNEL_NORM
DIAGONAL_SHIFT = 1.0
REACH = 4.0 / 3.0
CELL = REACH / 2.0
VMEM_BYTES = 67_043_328
SPARE = 8192
EARLY = 2
MESH = pl.DeviceIdType.MESH
DIRECTIONS = ((1, 0), (-1, 0), (0, 1), (0, -1), (1, 1), (-1, 1), (1, -1), (-1, -1))


def kernel(
    rows,
    cols,
    off_hbm,
    vel_hbm,
    mass_hbm,
    counts_hbm,
    low_hbm,
    high_hbm,
    nv_ref,
    press_ref,
    off_ref,
    vel_ref,
    mass_ref,
    counts_ref,
    low_ref,
    high_ref,
    input_sem,
    tile_ref,
    above_ref,
    edge_ref,
    beside_ref,
    bend_ref,
    corner_ref,
    near_ref,
    around_ref,
    slopes_ref,
    moment_ref,
    own_ref,
    send_sem,
    recv_sem,
):
    slots, height, width = mass_hbm.shape
    steps = height // 8
    span = width // steps
    strip, corners, tops = steps, steps + 1, steps + 2
    planes = 5 * slots
    batch = width // span
    my_row = lax.axis_index("row")
    my_col = lax.axis_index("col")

    def exists(dr, dc):
        answer = None
        for shift, place, length in ((dr, my_row, rows), (dc, my_col, cols)):
            if shift == 0:
                continue
            test = place + shift < length if shift > 0 else place + shift >= 0
            answer = test if answer is None else jnp.logical_and(answer, test)
        return answer

    lane = lax.broadcasted_iota(jnp.int32, (8, width), 1)
    line = lax.broadcasted_iota(jnp.int32, (8, width), 0)
    place = lane % span
    block = ((lane + span // 2) % width) // span
    left_half = place < span // 2
    inverse_at, diagonal_at, residual_at, moment_at, sum_at, step_at = 0, 1, 2, 3, 5, 6

    loads = [
        pltpu.make_async_copy(source, target, input_sem.at[n])
        for n, (source, target) in enumerate(
            (
                (counts_hbm, counts_ref),
                (vel_hbm, vel_ref),
                (off_hbm, off_ref),
                (mass_hbm, mass_ref),
                (low_hbm, low_ref),
                (high_hbm, high_ref),
            )
        )
    ]
    for load in loads:
        load.start()

    barrier = pltpu.get_barrier_semaphore()
    for dr, dc in DIRECTIONS:

        @pl.when(exists(dr, dc))
        def _(dr=dr, dc=dc):
            pl.semaphore_signal(
                barrier, inc=1, device_id=(my_row + dr, my_col + dc), device_id_type=MESH
            )

    for side, dr in ((0, -1), (1, 1)):

        @pl.when(jnp.logical_not(exists(dr, 0)))
        def _(side=side):
            above_ref[side] = jnp.zeros(above_ref.shape[1:], jnp.float32)

    for side, dc in ((0, -1), (1, 1)):

        @pl.when(jnp.logical_not(exists(0, dc)))
        def _(side=side):
            beside_ref[side] = jnp.zeros(beside_ref.shape[1:], jnp.float32)

        for level, dr in ((0, -1), (1, 1)):

            @pl.when(jnp.logical_not(exists(dr, dc)))
            def _(side=side, level=level):
                corner_ref[side, level] = jnp.zeros(corner_ref.shape[2:], jnp.float32)

    for load in loads:
        load.wait()

    def particles(window, put):
        live = counts_ref[window, :]
        for slot in range(slots):
            occupied = jnp.where(live > slot, 1.0, 0.0).astype(jnp.float32)
            for axis in range(2):
                speed = vel_ref[axis, slot, window, :]
                place = off_ref[axis, slot, window, :] + TIME_STEP * speed
                put(axis * slots + slot, CELL * place)
                put((2 + axis) * slots + slot, speed)
            weight = mass_ref[slot, window, :] * occupied
            put(4 * slots + slot, (SLOPE_NORM / REACH**3) * weight)

    def own_tile(s, carry):
        window = pl.ds(pl.multiple_of(8 * s, 8), 8)

        def put_tile(plane, value):
            tile_ref[plane, window, :] = value

        particles(window, put_tile)
        return carry

    lax.fori_loop(0, steps, own_tile, 0)

    def lane_roll(value, shift):
        shift = shift % width
        return pltpu.roll(value, shift, 1) if shift else value

    def under(value, shift):
        return pltpu.roll(value, shift % 8, 0)

    def edges(plane):
        packed = tile_ref[plane, 0:8, :]
        for s in range(1, steps):
            moved = lane_roll(tile_ref[plane, 8 * s : 8 * s + 8, :], span * s)
            packed = jnp.where(block == s, moved, packed)
        return packed

    def each_plane(work):
        def body(index, carry):
            for n in range(slots):
                work(index * slots + n)
            return carry

        lax.fori_loop(0, planes // slots, body, 0)

    def pack(plane):
        edge_ref[plane] = edges(plane)

    each_plane(pack)

    for level, home in ((0, steps - 1), (1, 0)):
        for g in range(bend_ref.shape[1]):
            packed = None
            for n in range(min(batch, planes - g * batch)):
                moved = lane_roll(edge_ref[g * batch + n], span * (n - home))
                packed = moved if packed is None else jnp.where(block == n, moved, packed)
            bend_ref[level, g] = packed

    def copy(way):
        dr, dc = DIRECTIONS[way]
        theirs = 0 if dc > 0 else 1
        if dc == 0 and dr > 0:
            source, target = tile_ref.at[:, height - 8 : height, :], above_ref.at[0]
        elif dc == 0:
            source, target = tile_ref.at[:, 0:8, :], above_ref.at[1]
        elif dr == 0:
            source, target = edge_ref, beside_ref.at[theirs]
        else:
            level = 0 if dr > 0 else 1
            source, target = bend_ref.at[level], corner_ref.at[theirs, level]
        return pltpu.make_async_remote_copy(
            src_ref=source,
            dst_ref=target,
            send_sem=send_sem.at[way],
            recv_sem=recv_sem.at[way],
            device_id=(my_row + dr, my_col + dc),
            device_id_type=MESH,
        )

    def own_line(plane):
        for t in range(steps):
            value = tile_ref[plane, pl.ds(t, 8, stride=8), :]
            for f in range(5):
                near_ref[f, plane, t + 2] = lane_roll(value, 2 - f)

    each_plane(own_line)

    def near_line(t):
        return lambda e, f, plane: near_ref[f, plane, t + e]

    def near_around(n):
        return lambda e, f, plane: around_ref[n, e, f, plane]

    def own(near, first):
        return jnp.stack([near(2, 2, first * slots + slot) for slot in range(slots)])

    zero = jnp.zeros((slots, 8, width), jnp.float32)
    def flow(x, near, low_e, high_e, sums, moments):
        own_x = own(near, 0)
        own_y = own(near, 1)
        if not moments:
            own_vx = own(near, 2)
            own_vy = own(near, 3)

        def along(e, sums):
            sums = list(sums)
            base_x = own_x - CELL * jnp.asarray(e - 2, jnp.float32)
            for f in range(5):
                base_y = own_y - CELL * (f - 2) if f != 2 else own_y
                for b in range(slots):
                    dx = near(e, f, b)[None] - base_x
                    dy = near(e, f, slots + b)[None] - base_y
                    square = dx * dx + dy * dy
                    inverse = lax.rsqrt(square)
                    dist = lax.rsqrt(inverse * inverse)
                    u = jnp.maximum(REACH - dist, 0.0)
                    slope = (u * u) * (near(e, f, 4 * slots + b)[None] * u)
                    slopes_ref[x * 5 + e, f, b] = slope
                    sums[0] = sums[0] + slope
                    sums[1] = sums[1] + slope * (dist - square)
                    if moments:
                        moment_ref[0, x * 5 + e, f, b] = slope * dx
                        moment_ref[1, x * 5 + e, f, b] = slope * dy
                    else:
                        dvx = near(e, f, 2 * slots + b)[None] - own_vx
                        dvy = near(e, f, 3 * slots + b)[None] - own_vy
                        sums[2] = sums[2] + slope * (dvx * dx + dvy * dy)
            return tuple(sums)

        return lax.fori_loop(low_e, high_e, along, sums)

    def stir(x, near):
        def along(e, sums):
            flux, sum_x, sum_y = sums
            for f in range(5):
                for b in range(slots):
                    moment_x = moment_ref[0, x * 5 + e, f, b]
                    moment_y = moment_ref[1, x * 5 + e, f, b]
                    flux = flux + moment_x * near(e, f, 2 * slots + b)[None]
                    flux = flux + moment_y * near(e, f, 3 * slots + b)[None]
                    sum_x = sum_x + moment_x
                    sum_y = sum_y + moment_y
            return flux, sum_x, sum_y

        flux, sum_x, sum_y = lax.fori_loop(0, 5, along, (zero,) * 3)
        own_ref[moment_at, x] = sum_x
        own_ref[moment_at + 1, x] = sum_y
        return flux - own(near, 2) * sum_x - own(near, 3) * sum_y

    def save(x, sums):
        for n, value in enumerate(sums):
            own_ref[n, x] = value

    def saved(x, count):
        return tuple(own_ref[n, x] for n in range(count))

    def each(first, last, work):
        def body(x, carry):
            work(x)
            return carry

        lax.fori_loop(first, last, body, 0)

    def flow_inner(t):
        low_e = jnp.maximum(0, 2 - t)
        high_e = jnp.minimum(5, steps + 2 - t)
        save(t, flow(t, near_line(t), low_e, high_e, (zero,) * 2, True))

    def flow_outer(index):
        t = index + (index // 2) * (steps - 4)
        low_e = jnp.where(t < 2, 0, steps + 2 - t)
        high_e = jnp.where(t < 2, 2 - t, 5)
        save(t, flow(t, near_line(t), low_e, high_e, saved(t, 2), True))

    each(0, EARLY, flow_inner)

    tall = 1 + jnp.where(my_row > 0, 1, 0) + jnp.where(my_row + 1 < rows, 1, 0)
    wide = 1 + jnp.where(my_col > 0, 1, 0) + jnp.where(my_col + 1 < cols, 1, 0)
    pl.semaphore_wait(barrier, tall * wide - 1)
    for way in (4, 5, 6, 7, 2, 3, 0, 1):

        @pl.when(exists(*DIRECTIONS[way]))
        def _(way=way):
            copy(way).start()

    each(EARLY, steps, flow_inner)


    for way in range(8):
        dr, dc = DIRECTIONS[way]

        @pl.when(exists(-dr, -dc))
        def _(way=way):
            copy(way).wait_recv()

    def ring(plane, top, bottom):
        for f in range(5):
            above, below = lane_roll(top, 2 - f), lane_roll(bottom, 2 - f)
            first, second = near_ref[f, plane, 2], near_ref[f, plane, 3]
            before, last = near_ref[f, plane, steps], near_ref[f, plane, steps + 1]
            near_ref[f, plane, 0] = jnp.where(line == 0, under(above, 2), under(before, 1))
            near_ref[f, plane, 1] = jnp.where(line == 0, under(above, 1), under(last, 1))
            near_ref[f, plane, steps + 2] = jnp.where(line == 7, under(below, 7), under(first, 7))
            near_ref[f, plane, steps + 3] = jnp.where(line == 7, under(below, 6), under(second, 7))
            around_ref[2, 0, f, plane] = under(above, 2)
            around_ref[2, 1, f, plane] = under(above, 1)
            around_ref[2, 2, f, plane] = above
            around_ref[2, 3, f, plane] = jnp.where(line == 7, under(first, 7), under(above, 7))
            beyond = jnp.where(line == 7, under(second, 7), under(above, 6))
            around_ref[2, 4, f, plane] = jnp.where(line == 6, under(first, 6), beyond)
            beyond = jnp.where(line == 1, under(last, 2), under(below, 2))
            around_ref[3, 0, f, plane] = jnp.where(line == 0, under(before, 1), beyond)
            around_ref[3, 1, f, plane] = jnp.where(line == 0, under(last, 1), under(below, 1))
            around_ref[3, 2, f, plane] = below
            around_ref[3, 3, f, plane] = under(below, 7)
            around_ref[3, 4, f, plane] = under(below, 6)

    def widen(plane, inner, outer):
        for f in range(5):
            mine = (lane + (span + 2 - f)) % span < span // 2
            here = lane_roll(jnp.where(mine, *inner), 2 - f)
            bend = lane_roll(jnp.where(mine, *outer), 2 - f)
            after = jnp.where(lane >= width - span, bend, lane_roll(here, -span))
            ahead = jnp.where(lane < span, bend, lane_roll(here, span))
            for n, value, up, down in ((0, here, after, ahead), (1, bend, here, here)):
                around_ref[n, 0, f, plane] = under(jnp.where(line >= 6, down, value), 2)
                around_ref[n, 1, f, plane] = under(jnp.where(line >= 7, down, value), 1)
                around_ref[n, 2, f, plane] = value
                around_ref[n, 3, f, plane] = under(jnp.where(line < 1, up, value), 7)
                around_ref[n, 4, f, plane] = under(jnp.where(line < 2, up, value), 6)

    def fold(top, bottom):
        return jnp.where(block == 0, top, lane_roll(bottom, span * (steps - 1)))

    def arrive(plane, g, n):
        top, bottom = above_ref[0, plane], above_ref[1, plane]
        ring(plane, top, bottom)

        def strips(mine, theirs):
            left = lane_roll(jnp.where(left_half, mine, theirs), 6)
            right = lane_roll(jnp.where(left_half, theirs, mine), 10)
            return left, right

        inner = jnp.where(left_half, beside_ref[1, plane], beside_ref[0, plane])
        ends = [jnp.where(left_half, corner_ref[1, level, g], corner_ref[0, level, g]) for level in (0, 1)]
        outer = fold(lane_roll(ends[0], -span * n), lane_roll(ends[1], -span * n))
        widen(plane, strips(edge_ref[plane], inner), strips(fold(top, bottom), outer))

    def arrive_some(index, carry):
        g = index // 2
        for half in range(2):

            @pl.when(index % 2 == half)
            def _(half=half):
                for n in range(slots):
                    arrive(index * slots + n, g, half * slots + n)

        return carry

    lax.fori_loop(0, planes // slots, arrive_some, 0)

    each(0, 4, flow_outer)
    save(strip, flow(strip, near_around(0), 0, 5, (zero,) * 2, True))
    each(1, 4, lambda n: save(steps + n, flow(steps + n, near_around(n), 0, 5, (zero,) * 3, False)))

    full = (8, width)
    low = jnp.broadcast_to(low_ref[0], full)
    high = jnp.broadcast_to(high_ref[0], full)
    middle = 0.5 * (high + low)
    radius = 0.5 * (high - low)
    quotient = middle / radius
    factor_zero = 1.0 / quotient
    factor_one = 1.0 / (2.0 * quotient - factor_zero)
    factor_two = 1.0 / (2.0 * quotient - factor_one)
    over_middle = 1.0 / middle
    keep_one = factor_one * factor_zero
    keep_two = factor_two * factor_one
    gain_one = 2.0 * factor_one / radius
    gain_two = 2.0 * factor_two / radius

    def everyone(work):
        each(0, steps, lambda t: work(t, near_line(t)))
        each(0, 4, lambda n: work(steps + n, near_around(n)))

    def first_step(x, slope_sum, dens, inflow):
        density = BACKGROUND + (KERNEL_NORM / SLOPE_NORM) * (slope_sum + (4.0 / REACH**2) * dens)
        inverse = 1.0 / density
        source = inflow * inverse * (-1.0 / (CELL * TIME_STEP))
        own_ref[inverse_at, x] = inverse
        own_ref[diagonal_at, x] = DIAGONAL_SHIFT + 2.0 * inverse * slope_sum
        own_ref[residual_at, x] = source
        own_ref[sum_at, x] = source * over_middle[None]

    def turn(value):
        return jnp.where(left_half, lane_roll(value, -2), lane_roll(value, 2))

    def mend(value, turned, s):
        outermost = (lane < 2) | (lane >= width - 2)
        return jnp.where(outermost, lane_roll(turned, -span * s - span // 2), value)

    def refresh(at):
        for slot in range(slots):
            for t in range(steps):
                tile_ref[slot, pl.ds(t, 8, stride=8), :] = own_ref[at, t, slot]
            inner, outer = own_ref[at, strip, slot], own_ref[at, corners, slot]
            turned = turn(inner)
            for s in range(steps):
                window = slice(8 * s, 8 * s + 8)
                tile_ref[slot, window, :] = mend(tile_ref[slot, window, :], turned, s)
            turned = turn(outer)
            top = mend(own_ref[at, tops, slot], turned, 0)
            bottom = mend(own_ref[at, tops + 1, slot], turned, steps - 1)
            own_line(slot)
            ring(slot, top, bottom)

            def strips(value, mine):
                left = jnp.where(left_half, value, lane_roll(mine, 6))
                right = jnp.where(left_half, lane_roll(mine, 10), value)
                return left, right

            widen(slot, strips(inner, edges(slot)), strips(outer, fold(top, bottom)))

    def gather(x, near):
        def along(e, totals):
            totals = list(totals)
            for f in range(5):
                for b in range(slots):
                    value = near(e, f, b)[None]
                    totals[b % 2] = totals[b % 2] + slopes_ref[x * 5 + e, f, b] * value
            return tuple(totals)

        even, odd = lax.fori_loop(0, 5, along, (zero, zero))
        return even + odd

    def improve(x, near, here):
        total = gather(x, near)
        change = own_ref[diagonal_at, x] * here - 2.0 * own_ref[inverse_at, x] * total
        residual = own_ref[residual_at, x] - change
        own_ref[residual_at, x] = residual
        return residual

    def second_step(x, near):
        here = own_ref[sum_at, x]
        own_ref[step_at, x] = keep_one[None] * here + gain_one[None] * improve(x, near, here)

    def third_step(x, near):
        here = own_ref[step_at, x]
        third = keep_two[None] * here + gain_two[None] * improve(x, near, here)
        own_ref[sum_at, x] = own_ref[sum_at, x] + here + third

    def push(x, near):
        def along(e, totals):
            push_x, push_y = totals
            for f in range(5):
                for b in range(slots):
                    value = near(e, f, b)[None]
                    push_x = push_x + moment_ref[0, x * 5 + e, f, b] * value
                    push_y = push_y + moment_ref[1, x * 5 + e, f, b] * value
            return push_x, push_y

        pushes = lax.fori_loop(0, 5, along, (zero, zero))
        solved = own_ref[sum_at, x]
        scale = own_ref[inverse_at, x] * (TIME_STEP / CELL)
        return [
            own(near, 2 + axis) - scale * (pushes[axis] - solved * own_ref[moment_at + axis, x])
            for axis in range(2)
        ]

    def kick_line(t):
        for axis, value in enumerate(push(t, near_line(t))):
            for slot in range(slots):
                nv_ref[axis, slot, pl.ds(t, 8, stride=8), :] = value[slot]

    def kick_ends():
        turned = [[turn(value[slot]) for slot in range(slots)] for value in push(strip, near_around(0))]
        for s in range(steps):
            window = slice(8 * s, 8 * s + 8)
            live = counts_ref[window, :]
            for slot in range(slots):
                occupied = jnp.where(live > slot, 1.0, 0.0).astype(jnp.float32)
                for axis in range(2):
                    value = mend(nv_ref[axis, slot, window, :], turned[axis][slot], s)
                    nv_ref[axis, slot, window, :] = occupied * value
                press_ref[slot, window, :] = occupied * tile_ref[slot, window, :]

    for way in range(8):

        @pl.when(exists(*DIRECTIONS[way]))
        def _(way=way):
            copy(way).wait_send()

    each(0, steps, lambda t: first_step(t, *saved(t, 2), stir(t, near_line(t))))
    first_step(strip, *saved(strip, 2), stir(strip, near_around(0)))
    each(1, 4, lambda n: first_step(steps + n, *saved(steps + n, 3)))
    refresh(sum_at)
    everyone(second_step)
    refresh(step_at)
    everyone(third_step)
    refresh(sum_at)
    each(0, steps, kick_line)
    kick_ends()

def on_device(rows, cols, offsets, velocity, mass, counts, spectrum_low, spectrum_high):
    slots, height, width = mass.shape
    steps = height // 8
    span = width // steps
    assert height % 8 == 0 and steps == 8 and width % 128 == 0 and span == 16
    planes = 5 * slots
    bends = -(-planes * span // width)
    count = steps + 4
    room_out = 4 * (velocity.size + mass.size)
    vmem = pl.BlockSpec(memory_space=pltpu.VMEM)
    hbm = pl.BlockSpec(memory_space=pltpu.HBM)

    def room(*shape):
        return pltpu.VMEM(shape, jnp.float32)

    results = pl.pallas_call(
        functools.partial(kernel, rows, cols),
        out_shape=(
            pltpu.VMEM(velocity.shape, jnp.float32),
            pltpu.VMEM(mass.shape, jnp.float32),
        ),
        in_specs=[hbm] * 6,
        out_specs=(vmem, vmem),
        scratch_shapes=[
            room(*offsets.shape),
            room(*velocity.shape),
            room(*mass.shape),
            pltpu.VMEM(counts.shape, jnp.int32),
            pltpu.SMEM(spectrum_low.shape, jnp.float32),
            pltpu.SMEM(spectrum_high.shape, jnp.float32),
            pltpu.SemaphoreType.DMA((6,)),
            room(planes, height, width),
            room(2, planes, 8, width),
            room(planes, 8, width),
            room(2, planes, 8, width),
            room(2, bends, 8, width),
            room(2, 2, bends, 8, width),
            room(5, planes, steps + 4, 8, width),
            room(4, 5, 5, planes, 8, width),
            room(count * 5, 5, slots, slots, 8, width),
            room(2, (steps + 1) * 5, 5, slots, slots, 8, width),
            room(7, count, slots, 8, width),
            pltpu.SemaphoreType.DMA((8,)),
            pltpu.SemaphoreType.DMA((8,)),
        ],
        compiler_params=pltpu.CompilerParams(
            collective_id=0,
            has_side_effects=True,
            vmem_limit_bytes=VMEM_BYTES - room_out - SPARE,
        ),
        name="sph_step",
    )(offsets, velocity, mass, counts, spectrum_low, spectrum_high)
    return pl.pallas_call(
        put_out,
        out_shape=(
            jax.ShapeDtypeStruct(velocity.shape, jnp.float32),
            jax.ShapeDtypeStruct(mass.shape, jnp.float32),
        ),
        in_specs=[vmem] * 2,
        out_specs=(hbm, hbm),
        scratch_shapes=[pltpu.SemaphoreType.DMA((2,))],
        compiler_params=pltpu.CompilerParams(vmem_limit_bytes=1 << 20),
        name="put_out",
    )(*results)


def put_out(nv_ref, press_ref, nv_hbm, press_hbm, sem):
    copies = [
        pltpu.make_async_copy(nv_ref, nv_hbm, sem.at[0]),
        pltpu.make_async_copy(press_ref, press_hbm, sem.at[1]),
    ]
    for copy in copies:
        copy.start()
    for copy in copies:
        copy.wait()


def solution(mesh):
    placed = (
        P(None, None, "row", "col"),
        P(None, None, "row", "col"),
        P(None, "row", "col"),
        P("row", "col"),
        P(),
        P(),
    )
    return jax.shard_map(
        functools.partial(on_device, mesh.shape["row"], mesh.shape["col"]),
        mesh=mesh,
        in_specs=placed,
        out_specs=(P(None, None, "row", "col"), P(None, "row", "col")),
        check_vma=False,
    )
```

```python
import functools
import math

import jax
import jax.numpy as jnp
from jax import lax
from jax.experimental import pallas as pl
from jax.experimental.pallas import tpu as pltpu
from jax.sharding import PartitionSpec as P

TIME_STEP = 0.1
KERNEL_NORM = 7.0 / (4.0 * math.pi)
SLOPE_NORM = 20.0 * KERNEL_NORM / 4.0
BACKGROUND = 0.5 * KERNEL_NORM
DIAGONAL_SHIFT = 1.0
REACH = 4.0 / 3.0
CELL = REACH / 2.0
VMEM_BYTES = 67_043_328
SPARE = 8192
EARLY = 2
MESH = pl.DeviceIdType.MESH
DIRECTIONS = ((1, 0), (-1, 0), (0, 1), (0, -1), (1, 1), (-1, 1), (1, -1), (-1, -1))


def kernel(
    rows,
    cols,
    off_hbm,
    vel_hbm,
    mass_hbm,
    counts_hbm,
    low_hbm,
    high_hbm,
    nv_ref,
    press_ref,
    off_ref,
    vel_ref,
    mass_ref,
    counts_ref,
    low_ref,
    high_ref,
    input_sem,
    tile_ref,
    above_ref,
    edge_ref,
    beside_ref,
    bend_ref,
    corner_ref,
    near_ref,
    around_ref,
    slopes_ref,
    moment_ref,
    own_ref,
    send_sem,
    recv_sem,
):
    slots, height, width = mass_hbm.shape
    steps = height // 8
    span = width // steps
    strip, corners, tops = steps, steps + 1, steps + 2
    planes = 5 * slots
    batch = width // span
    my_row = lax.axis_index("row")
    my_col = lax.axis_index("col")

    def exists(dr, dc):
        answer = None
        for shift, place, length in ((dr, my_row, rows), (dc, my_col, cols)):
            if shift == 0:
                continue
            test = place + shift < length if shift > 0 else place + shift >= 0
            answer = test if answer is None else jnp.logical_and(answer, test)
        return answer

    lane = lax.broadcasted_iota(jnp.int32, (8, width), 1)
    line = lax.broadcasted_iota(jnp.int32, (8, width), 0)
    place = lane % span
    block = ((lane + span // 2) % width) // span
    left_half = place < span // 2
    inverse_at, diagonal_at, residual_at, moment_at, sum_at, step_at = 0, 1, 2, 3, 5, 6

    loads = [
        pltpu.make_async_copy(source, target, input_sem.at[n])
        for n, (source, target) in enumerate(
            (
                (counts_hbm, counts_ref),
                (vel_hbm, vel_ref),
                (off_hbm, off_ref),
                (mass_hbm, mass_ref),
                (low_hbm, low_ref),
                (high_hbm, high_ref),
            )
        )
    ]
    for load in loads:
        load.start()

    barrier = pltpu.get_barrier_semaphore()
    for dr, dc in DIRECTIONS:

        @pl.when(exists(dr, dc))
        def _(dr=dr, dc=dc):
            pl.semaphore_signal(
                barrier, inc=1, device_id=(my_row + dr, my_col + dc), device_id_type=MESH
            )

    for side, dr in ((0, -1), (1, 1)):

        @pl.when(jnp.logical_not(exists(dr, 0)))
        def _(side=side):
            above_ref[side] = jnp.zeros(above_ref.shape[1:], jnp.float32)

    for side, dc in ((0, -1), (1, 1)):

        @pl.when(jnp.logical_not(exists(0, dc)))
        def _(side=side):
            beside_ref[side] = jnp.zeros(beside_ref.shape[1:], jnp.float32)

        for level, dr in ((0, -1), (1, 1)):

            @pl.when(jnp.logical_not(exists(dr, dc)))
            def _(side=side, level=level):
                corner_ref[side, level] = jnp.zeros(corner_ref.shape[2:], jnp.float32)

    for load in loads:
        load.wait()

    def particles(window, put):
        live = counts_ref[window, :]
        for slot in range(slots):
            occupied = jnp.where(live > slot, 1.0, 0.0).astype(jnp.float32)
            for axis in range(2):
                speed = vel_ref[axis, slot, window, :]
                place = off_ref[axis, slot, window, :] + TIME_STEP * speed
                put(axis * slots + slot, CELL * place)
                put((2 + axis) * slots + slot, speed)
            weight = mass_ref[slot, window, :] * occupied
            put(4 * slots + slot, (SLOPE_NORM / REACH**3) * weight)

    def own_tile(s, carry):
        window = pl.ds(pl.multiple_of(8 * s, 8), 8)

        def put_tile(plane, value):
            tile_ref[plane, window, :] = value

        particles(window, put_tile)
        return carry

    lax.fori_loop(0, steps, own_tile, 0)

    def lane_roll(value, shift):
        shift = shift % width
        return pltpu.roll(value, shift, 1) if shift else value

    def under(value, shift):
        return pltpu.roll(value, shift % 8, 0)

    def edges(plane):
        packed = tile_ref[plane, 0:8, :]
        for s in range(1, steps):
            moved = lane_roll(tile_ref[plane, 8 * s : 8 * s + 8, :], span * s)
            packed = jnp.where(block == s, moved, packed)
        return packed

    def bias_of(index):
        return jnp.where(index == 1, CELL, 0.0).astype(jnp.float32)

    def each_plane(work):
        def body(index, carry):
            for n in range(slots):
                work(index * slots + n)
            return carry

        lax.fori_loop(0, planes // slots, body, 0)

    def pack(plane):
        edge_ref[plane] = edges(plane)

    each_plane(pack)

    for level, home in ((0, steps - 1), (1, 0)):
        for g in range(bend_ref.shape[1]):
            packed = None
            for n in range(min(batch, planes - g * batch)):
                moved = lane_roll(edge_ref[g * batch + n], span * (n - home))
                packed = moved if packed is None else jnp.where(block == n, moved, packed)
            bend_ref[level, g] = packed

    def copy(way):
        dr, dc = DIRECTIONS[way]
        theirs = 0 if dc > 0 else 1
        if dc == 0 and dr > 0:
            source, target = tile_ref.at[:, height - 8 : height, :], above_ref.at[0]
        elif dc == 0:
            source, target = tile_ref.at[:, 0:8, :], above_ref.at[1]
        elif dr == 0:
            source, target = edge_ref, beside_ref.at[theirs]
        else:
            level = 0 if dr > 0 else 1
            source, target = bend_ref.at[level], corner_ref.at[theirs, level]
        return pltpu.make_async_remote_copy(
            src_ref=source,
            dst_ref=target,
            send_sem=send_sem.at[way],
            recv_sem=recv_sem.at[way],
            device_id=(my_row + dr, my_col + dc),
            device_id_type=MESH,
        )

    def shifted(value, f, bias):
        moved = lane_roll(value, 2 - f)
        return moved if bias is None or f == 2 else moved + bias * (f - 2.0)

    def own_line(plane, bias):
        for t in range(steps):
            value = tile_ref[plane, pl.ds(t, 8, stride=8), :]
            for f in range(5):
                near_ref[f, plane, t + 2] = shifted(value, f, bias)

    def own_lines(index, carry):
        for n in range(slots):
            own_line(index * slots + n, bias_of(index))
        return carry

    lax.fori_loop(0, planes // slots, own_lines, 0)

    def near_line(t):
        return lambda e, f, plane: near_ref[f, plane, t + e]

    def near_around(n):
        return lambda e, f, plane: around_ref[n, e, f, plane]

    def own(near, first):
        return jnp.stack([near(2, 2, first * slots + slot) for slot in range(slots)])

    zero = jnp.zeros((slots, 8, width), jnp.float32)
    def flow(x, near, low_e, high_e, sums, moments):
        own_x = own(near, 0)
        own_y = own(near, 1)
        if not moments:
            own_vx = own(near, 2)
            own_vy = own(near, 3)

        def along(e, sums):
            sums = list(sums)
            base_x = own_x - CELL * jnp.asarray(e - 2, jnp.float32)
            for f in range(5):
                for b in range(slots):
                    dx = near(e, f, b)[None] - base_x
                    dy = near(e, f, slots + b)[None] - own_y
                    square = dx * dx + dy * dy
                    inverse = lax.rsqrt(square)
                    dist = lax.rsqrt(inverse * inverse)
                    u = jnp.maximum(REACH - dist, 0.0)
                    slope = (u * u) * (near(e, f, 4 * slots + b)[None] * u)
                    slopes_ref[x * 5 + e, f, b] = slope
                    sums[0] = sums[0] + slope
                    sums[1] = sums[1] + slope * (dist - square)
                    if moments:
                        moment_ref[0, x * 5 + e, f, b] = slope * dx
                        moment_ref[1, x * 5 + e, f, b] = slope * dy
                    else:
                        dvx = near(e, f, 2 * slots + b)[None] - own_vx
                        dvy = near(e, f, 3 * slots + b)[None] - own_vy
                        sums[2] = sums[2] + slope * (dvx * dx + dvy * dy)
            return tuple(sums)

        return lax.fori_loop(low_e, high_e, along, sums)

    def stir(x, near):
        def along(e, sums):
            flux, sum_x, sum_y = sums
            for f in range(5):
                for b in range(slots):
                    moment_x = moment_ref[0, x * 5 + e, f, b]
                    moment_y = moment_ref[1, x * 5 + e, f, b]
                    flux = flux + moment_x * near(e, f, 2 * slots + b)[None]
                    flux = flux + moment_y * near(e, f, 3 * slots + b)[None]
                    sum_x = sum_x + moment_x
                    sum_y = sum_y + moment_y
            return flux, sum_x, sum_y

        flux, sum_x, sum_y = lax.fori_loop(0, 5, along, (zero,) * 3)
        own_ref[moment_at, x] = sum_x
        own_ref[moment_at + 1, x] = sum_y
        return flux - own(near, 2) * sum_x - own(near, 3) * sum_y

    def save(x, sums):
        for n, value in enumerate(sums):
            own_ref[n, x] = value

    def saved(x, count):
        return tuple(own_ref[n, x] for n in range(count))

    def each(first, last, work):
        def body(x, carry):
            work(x)
            return carry

        lax.fori_loop(first, last, body, 0)

    def flow_inner(t):
        low_e = jnp.maximum(0, 2 - t)
        high_e = jnp.minimum(5, steps + 2 - t)
        save(t, flow(t, near_line(t), low_e, high_e, (zero,) * 2, True))

    def flow_outer(index):
        t = index + (index // 2) * (steps - 4)
        low_e = jnp.where(t < 2, 0, steps + 2 - t)
        high_e = jnp.where(t < 2, 2 - t, 5)
        save(t, flow(t, near_line(t), low_e, high_e, saved(t, 2), True))

    each(0, EARLY, flow_inner)

    tall = 1 + jnp.where(my_row > 0, 1, 0) + jnp.where(my_row + 1 < rows, 1, 0)
    wide = 1 + jnp.where(my_col > 0, 1, 0) + jnp.where(my_col + 1 < cols, 1, 0)
    pl.semaphore_wait(barrier, tall * wide - 1)
    for way in (4, 5, 6, 7, 2, 3, 0, 1):

        @pl.when(exists(*DIRECTIONS[way]))
        def _(way=way):
            copy(way).start()

    each(EARLY, steps, flow_inner)


    for way in range(8):
        dr, dc = DIRECTIONS[way]

        @pl.when(exists(-dr, -dc))
        def _(way=way):
            copy(way).wait_recv()

    def ring(plane, top, bottom, bias):
        for f in range(5):
            above, below = shifted(top, f, bias), shifted(bottom, f, bias)
            first, second = near_ref[f, plane, 2], near_ref[f, plane, 3]
            before, last = near_ref[f, plane, steps], near_ref[f, plane, steps + 1]
            near_ref[f, plane, 0] = jnp.where(line == 0, under(above, 2), under(before, 1))
            near_ref[f, plane, 1] = jnp.where(line == 0, under(above, 1), under(last, 1))
            near_ref[f, plane, steps + 2] = jnp.where(line == 7, under(below, 7), under(first, 7))
            near_ref[f, plane, steps + 3] = jnp.where(line == 7, under(below, 6), under(second, 7))
            around_ref[2, 0, f, plane] = under(above, 2)
            around_ref[2, 1, f, plane] = under(above, 1)
            around_ref[2, 2, f, plane] = above
            around_ref[2, 3, f, plane] = jnp.where(line == 7, under(first, 7), under(above, 7))
            beyond = jnp.where(line == 7, under(second, 7), under(above, 6))
            around_ref[2, 4, f, plane] = jnp.where(line == 6, under(first, 6), beyond)
            beyond = jnp.where(line == 1, under(last, 2), under(below, 2))
            around_ref[3, 0, f, plane] = jnp.where(line == 0, under(before, 1), beyond)
            around_ref[3, 1, f, plane] = jnp.where(line == 0, under(last, 1), under(below, 1))
            around_ref[3, 2, f, plane] = below
            around_ref[3, 3, f, plane] = under(below, 7)
            around_ref[3, 4, f, plane] = under(below, 6)

    def widen(plane, inner, outer, bias):
        for f in range(5):
            mine = (lane + (span + 2 - f)) % span < span // 2
            here = shifted(jnp.where(mine, *inner), f, bias)
            bend = shifted(jnp.where(mine, *outer), f, bias)
            after = jnp.where(lane >= width - span, bend, lane_roll(here, -span))
            ahead = jnp.where(lane < span, bend, lane_roll(here, span))
            for n, value, up, down in ((0, here, after, ahead), (1, bend, here, here)):
                around_ref[n, 0, f, plane] = under(jnp.where(line >= 6, down, value), 2)
                around_ref[n, 1, f, plane] = under(jnp.where(line >= 7, down, value), 1)
                around_ref[n, 2, f, plane] = value
                around_ref[n, 3, f, plane] = under(jnp.where(line < 1, up, value), 7)
                around_ref[n, 4, f, plane] = under(jnp.where(line < 2, up, value), 6)

    def fold(top, bottom):
        return jnp.where(block == 0, top, lane_roll(bottom, span * (steps - 1)))

    def arrive(plane, g, n, bias):
        top, bottom = above_ref[0, plane], above_ref[1, plane]
        ring(plane, top, bottom, bias)

        def strips(mine, theirs):
            left = lane_roll(jnp.where(left_half, mine, theirs), 6)
            right = lane_roll(jnp.where(left_half, theirs, mine), 10)
            return left, right

        inner = jnp.where(left_half, beside_ref[1, plane], beside_ref[0, plane])
        ends = [jnp.where(left_half, corner_ref[1, level, g], corner_ref[0, level, g]) for level in (0, 1)]
        outer = fold(lane_roll(ends[0], -span * n), lane_roll(ends[1], -span * n))
        widen(plane, strips(edge_ref[plane], inner), strips(fold(top, bottom), outer), bias)

    def arrive_some(index, carry):
        g = index // 2
        for half in range(2):

            @pl.when(index % 2 == half)
            def _(half=half):
                for n in range(slots):
                    arrive(index * slots + n, g, half * slots + n, bias_of(index))

        return carry

    lax.fori_loop(0, planes // slots, arrive_some, 0)

    each(0, 4, flow_outer)
    save(strip, flow(strip, near_around(0), 0, 5, (zero,) * 2, True))
    each(1, 4, lambda n: save(steps + n, flow(steps + n, near_around(n), 0, 5, (zero,) * 3, False)))

    full = (8, width)
    low = jnp.broadcast_to(low_ref[0], full)
    high = jnp.broadcast_to(high_ref[0], full)
    middle = 0.5 * (high + low)
    radius = 0.5 * (high - low)
    quotient = middle / radius
    factor_zero = 1.0 / quotient
    factor_one = 1.0 / (2.0 * quotient - factor_zero)
    factor_two = 1.0 / (2.0 * quotient - factor_one)
    over_middle = 1.0 / middle
    keep_one = factor_one * factor_zero
    keep_two = factor_two * factor_one
    gain_one = 2.0 * factor_one / radius
    gain_two = 2.0 * factor_two / radius

    def everyone(work):
        each(0, steps, lambda t: work(t, near_line(t)))
        each(0, 4, lambda n: work(steps + n, near_around(n)))

    def first_step(x, slope_sum, dens, inflow):
        density = BACKGROUND + (KERNEL_NORM / SLOPE_NORM) * (slope_sum + (4.0 / REACH**2) * dens)
        inverse = 1.0 / density
        source = inflow * inverse * (-1.0 / (CELL * TIME_STEP))
        own_ref[inverse_at, x] = inverse
        own_ref[diagonal_at, x] = DIAGONAL_SHIFT + 2.0 * inverse * slope_sum
        own_ref[residual_at, x] = source
        own_ref[sum_at, x] = source * over_middle[None]

    def turn(value):
        return jnp.where(left_half, lane_roll(value, -2), lane_roll(value, 2))

    def mend(value, turned, s):
        outermost = (lane < 2) | (lane >= width - 2)
        return jnp.where(outermost, lane_roll(turned, -span * s - span // 2), value)

    def refresh(at):
        for slot in range(slots):
            for t in range(steps):
                tile_ref[slot, pl.ds(t, 8, stride=8), :] = own_ref[at, t, slot]
            inner, outer = own_ref[at, strip, slot], own_ref[at, corners, slot]
            turned = turn(inner)
            for s in range(steps):
                window = slice(8 * s, 8 * s + 8)
                tile_ref[slot, window, :] = mend(tile_ref[slot, window, :], turned, s)
            turned = turn(outer)
            top = mend(own_ref[at, tops, slot], turned, 0)
            bottom = mend(own_ref[at, tops + 1, slot], turned, steps - 1)
            own_line(slot, None)
            ring(slot, top, bottom, None)

            def strips(value, mine):
                left = jnp.where(left_half, value, lane_roll(mine, 6))
                right = jnp.where(left_half, lane_roll(mine, 10), value)
                return left, right

            widen(slot, strips(inner, edges(slot)), strips(outer, fold(top, bottom)), None)

    def gather(x, near):
        def along(e, totals):
            totals = list(totals)
            for f in range(5):
                for b in range(slots):
                    value = near(e, f, b)[None]
                    totals[b % 2] = totals[b % 2] + slopes_ref[x * 5 + e, f, b] * value
            return tuple(totals)

        even, odd = lax.fori_loop(0, 5, along, (zero, zero))
        return even + odd

    def improve(x, near, here):
        total = gather(x, near)
        change = own_ref[diagonal_at, x] * here - 2.0 * own_ref[inverse_at, x] * total
        residual = own_ref[residual_at, x] - change
        own_ref[residual_at, x] = residual
        return residual

    def second_step(x, near):
        here = own_ref[sum_at, x]
        own_ref[step_at, x] = keep_one[None] * here + gain_one[None] * improve(x, near, here)

    def third_step(x, near):
        here = own_ref[step_at, x]
        third = keep_two[None] * here + gain_two[None] * improve(x, near, here)
        own_ref[sum_at, x] = own_ref[sum_at, x] + here + third

    def push(x, near):
        def along(e, totals):
            push_x, push_y = totals
            for f in range(5):
                for b in range(slots):
                    value = near(e, f, b)[None]
                    push_x = push_x + moment_ref[0, x * 5 + e, f, b] * value
                    push_y = push_y + moment_ref[1, x * 5 + e, f, b] * value
            return push_x, push_y

        pushes = lax.fori_loop(0, 5, along, (zero, zero))
        solved = own_ref[sum_at, x]
        scale = own_ref[inverse_at, x] * (TIME_STEP / CELL)
        return [
            own(near, 2 + axis) - scale * (pushes[axis] - solved * own_ref[moment_at + axis, x])
            for axis in range(2)
        ]

    def kick_line(t):
        for axis, value in enumerate(push(t, near_line(t))):
            for slot in range(slots):
                nv_ref[axis, slot, pl.ds(t, 8, stride=8), :] = value[slot]

    def kick_ends():
        turned = [[turn(value[slot]) for slot in range(slots)] for value in push(strip, near_around(0))]
        for s in range(steps):
            window = slice(8 * s, 8 * s + 8)
            live = counts_ref[window, :]
            for slot in range(slots):
                occupied = jnp.where(live > slot, 1.0, 0.0).astype(jnp.float32)
                for axis in range(2):
                    value = mend(nv_ref[axis, slot, window, :], turned[axis][slot], s)
                    nv_ref[axis, slot, window, :] = occupied * value
                press_ref[slot, window, :] = occupied * tile_ref[slot, window, :]

    for way in range(8):

        @pl.when(exists(*DIRECTIONS[way]))
        def _(way=way):
            copy(way).wait_send()

    each(0, steps, lambda t: first_step(t, *saved(t, 2), stir(t, near_line(t))))
    first_step(strip, *saved(strip, 2), stir(strip, near_around(0)))
    each(1, 4, lambda n: first_step(steps + n, *saved(steps + n, 3)))
    refresh(sum_at)
    everyone(second_step)
    refresh(step_at)
    everyone(third_step)
    refresh(sum_at)
    each(0, steps, kick_line)
    kick_ends()

def on_device(rows, cols, offsets, velocity, mass, counts, spectrum_low, spectrum_high):
    slots, height, width = mass.shape
    steps = height // 8
    span = width // steps
    assert height % 8 == 0 and steps == 8 and width % 128 == 0 and span == 16
    planes = 5 * slots
    bends = -(-planes * span // width)
    count = steps + 4
    room_out = 4 * (velocity.size + mass.size)
    vmem = pl.BlockSpec(memory_space=pltpu.VMEM)
    hbm = pl.BlockSpec(memory_space=pltpu.HBM)

    def room(*shape):
        return pltpu.VMEM(shape, jnp.float32)

    results = pl.pallas_call(
        functools.partial(kernel, rows, cols),
        out_shape=(
            pltpu.VMEM(velocity.shape, jnp.float32),
            pltpu.VMEM(mass.shape, jnp.float32),
        ),
        in_specs=[hbm] * 6,
        out_specs=(vmem, vmem),
        scratch_shapes=[
            room(*offsets.shape),
            room(*velocity.shape),
            room(*mass.shape),
            pltpu.VMEM(counts.shape, jnp.int32),
            pltpu.SMEM(spectrum_low.shape, jnp.float32),
            pltpu.SMEM(spectrum_high.shape, jnp.float32),
            pltpu.SemaphoreType.DMA((6,)),
            room(planes, height, width),
            room(2, planes, 8, width),
            room(planes, 8, width),
            room(2, planes, 8, width),
            room(2, bends, 8, width),
            room(2, 2, bends, 8, width),
            room(5, planes, steps + 4, 8, width),
            room(4, 5, 5, planes, 8, width),
            room(count * 5, 5, slots, slots, 8, width),
            room(2, (steps + 1) * 5, 5, slots, slots, 8, width),
            room(7, count, slots, 8, width),
            pltpu.SemaphoreType.DMA((8,)),
            pltpu.SemaphoreType.DMA((8,)),
        ],
        compiler_params=pltpu.CompilerParams(
            collective_id=0,
            has_side_effects=True,
            vmem_limit_bytes=VMEM_BYTES - room_out - SPARE,
        ),
        name="sph_step",
    )(offsets, velocity, mass, counts, spectrum_low, spectrum_high)
    return pl.pallas_call(
        put_out,
        out_shape=(
            jax.ShapeDtypeStruct(velocity.shape, jnp.float32),
            jax.ShapeDtypeStruct(mass.shape, jnp.float32),
        ),
        in_specs=[vmem] * 2,
        out_specs=(hbm, hbm),
        scratch_shapes=[pltpu.SemaphoreType.DMA((2,))],
        compiler_params=pltpu.CompilerParams(vmem_limit_bytes=1 << 20),
        name="put_out",
    )(*results)


def put_out(nv_ref, press_ref, nv_hbm, press_hbm, sem):
    copies = [
        pltpu.make_async_copy(nv_ref, nv_hbm, sem.at[0]),
        pltpu.make_async_copy(press_ref, press_hbm, sem.at[1]),
    ]
    for copy in copies:
        copy.start()
    for copy in copies:
        copy.wait()


def solution(mesh):
    placed = (
        P(None, None, "row", "col"),
        P(None, None, "row", "col"),
        P(None, "row", "col"),
        P("row", "col"),
        P(),
        P(),
    )
    return jax.shard_map(
        functools.partial(on_device, mesh.shape["row"], mesh.shape["col"]),
        mesh=mesh,
        in_specs=placed,
        out_specs=(P(None, None, "row", "col"), P(None, "row", "col")),
        check_vma=False,
    )
```

```python
import functools
import math

import jax
import jax.numpy as jnp
from jax import lax
from jax.experimental import pallas as pl
from jax.experimental.pallas import tpu as pltpu
from jax.sharding import PartitionSpec as P

TIME_STEP = 0.1
KERNEL_NORM = 7.0 / (4.0 * math.pi)
SLOPE_NORM = 20.0 * KERNEL_NORM / 4.0
BACKGROUND = 0.5 * KERNEL_NORM
DIAGONAL_SHIFT = 1.0
REACH = 4.0 / 3.0
CELL = REACH / 2.0
VMEM_BYTES = 67_043_328
SPARE = 8192
EARLY = 2
MESH = pl.DeviceIdType.MESH
DIRECTIONS = ((1, 0), (-1, 0), (0, 1), (0, -1), (1, 1), (-1, 1), (1, -1), (-1, -1))


def kernel(
    rows,
    cols,
    off_hbm,
    vel_hbm,
    mass_hbm,
    counts_hbm,
    low_hbm,
    high_hbm,
    nv_ref,
    press_ref,
    off_ref,
    vel_ref,
    mass_ref,
    counts_ref,
    low_ref,
    high_ref,
    input_sem,
    tile_ref,
    above_ref,
    edge_ref,
    beside_ref,
    bend_ref,
    corner_ref,
    near_ref,
    around_ref,
    slopes_ref,
    moment_ref,
    own_ref,
    send_sem,
    recv_sem,
):
    slots, height, width = mass_hbm.shape
    steps = height // 8
    span = width // steps
    strip, corners, tops = steps, steps + 1, steps + 2
    planes = 5 * slots
    batch = width // span
    my_row = lax.axis_index("row")
    my_col = lax.axis_index("col")

    def exists(dr, dc):
        answer = None
        for shift, place, length in ((dr, my_row, rows), (dc, my_col, cols)):
            if shift == 0:
                continue
            test = place + shift < length if shift > 0 else place + shift >= 0
            answer = test if answer is None else jnp.logical_and(answer, test)
        return answer

    lane = lax.broadcasted_iota(jnp.int32, (8, width), 1)
    line = lax.broadcasted_iota(jnp.int32, (8, width), 0)
    place = lane % span
    block = ((lane + span // 2) % width) // span
    left_half = place < span // 2
    inverse_at, diagonal_at, residual_at, moment_at, sum_at, step_at = 0, 1, 2, 3, 5, 6

    loads = [
        pltpu.make_async_copy(source, target, input_sem.at[n])
        for n, (source, target) in enumerate(
            (
                (counts_hbm, counts_ref),
                (vel_hbm, vel_ref),
                (off_hbm, off_ref),
                (mass_hbm, mass_ref),
                (low_hbm, low_ref),
                (high_hbm, high_ref),
            )
        )
    ]
    for load in loads:
        load.start()

    barrier = pltpu.get_barrier_semaphore()
    for dr, dc in DIRECTIONS:

        @pl.when(exists(dr, dc))
        def _(dr=dr, dc=dc):
            pl.semaphore_signal(
                barrier, inc=1, device_id=(my_row + dr, my_col + dc), device_id_type=MESH
            )

    for side, dr in ((0, -1), (1, 1)):

        @pl.when(jnp.logical_not(exists(dr, 0)))
        def _(side=side):
            above_ref[side] = jnp.zeros(above_ref.shape[1:], jnp.float32)

    for side, dc in ((0, -1), (1, 1)):

        @pl.when(jnp.logical_not(exists(0, dc)))
        def _(side=side):
            beside_ref[side] = jnp.zeros(beside_ref.shape[1:], jnp.float32)

        for level, dr in ((0, -1), (1, 1)):

            @pl.when(jnp.logical_not(exists(dr, dc)))
            def _(side=side, level=level):
                corner_ref[side, level] = jnp.zeros(corner_ref.shape[2:], jnp.float32)

    for load in loads:
        load.wait()

    def particles(window, put):
        live = counts_ref[window, :]
        for slot in range(slots):
            occupied = jnp.where(live > slot, 1.0, 0.0).astype(jnp.float32)
            for axis in range(2):
                speed = vel_ref[axis, slot, window, :]
                place = off_ref[axis, slot, window, :] + TIME_STEP * speed
                put(axis * slots + slot, CELL * place)
                put((2 + axis) * slots + slot, speed)
            weight = mass_ref[slot, window, :] * occupied
            put(4 * slots + slot, (SLOPE_NORM / REACH**3) * weight)

    def own_tile(s, carry):
        window = pl.ds(pl.multiple_of(8 * s, 8), 8)

        def put_tile(plane, value):
            tile_ref[plane, window, :] = value

        particles(window, put_tile)
        return carry

    lax.fori_loop(0, steps, own_tile, 0)

    def lane_roll(value, shift):
        shift = shift % width
        return pltpu.roll(value, shift, 1) if shift else value

    def under(value, shift):
        return pltpu.roll(value, shift % 8, 0)

    def edges(plane):
        packed = tile_ref[plane, 0:8, :]
        for s in range(1, steps):
            moved = lane_roll(tile_ref[plane, 8 * s : 8 * s + 8, :], span * s)
            packed = jnp.where(block == s, moved, packed)
        return packed

    def bias_of(index):
        return jnp.where(index == 1, CELL, 0.0).astype(jnp.float32)

    def each_plane(work):
        def body(index, carry):
            for n in range(slots):
                work(index * slots + n)
            return carry

        lax.fori_loop(0, planes // slots, body, 0)

    def pack(plane):
        edge_ref[plane] = edges(plane)

    each_plane(pack)

    for level, home in ((0, steps - 1), (1, 0)):
        for g in range(bend_ref.shape[1]):
            packed = None
            for n in range(min(batch, planes - g * batch)):
                moved = lane_roll(edge_ref[g * batch + n], span * (n - home))
                packed = moved if packed is None else jnp.where(block == n, moved, packed)
            bend_ref[level, g] = packed

    def copy(way):
        dr, dc = DIRECTIONS[way]
        theirs = 0 if dc > 0 else 1
        if dc == 0 and dr > 0:
            source, target = tile_ref.at[:, height - 8 : height, :], above_ref.at[0]
        elif dc == 0:
            source, target = tile_ref.at[:, 0:8, :], above_ref.at[1]
        elif dr == 0:
            source, target = edge_ref, beside_ref.at[theirs]
        else:
            level = 0 if dr > 0 else 1
            source, target = bend_ref.at[level], corner_ref.at[theirs, level]
        return pltpu.make_async_remote_copy(
            src_ref=source,
            dst_ref=target,
            send_sem=send_sem.at[way],
            recv_sem=recv_sem.at[way],
            device_id=(my_row + dr, my_col + dc),
            device_id_type=MESH,
        )

    def shifted(value, f, bias):
        moved = lane_roll(value, 2 - f)
        return moved if bias is None or f == 2 else moved + bias * (f - 2.0)

    def own_line(plane, bias):
        for t in range(steps):
            value = tile_ref[plane, pl.ds(t, 8, stride=8), :]
            for f in range(5):
                near_ref[f, plane, t + 2] = shifted(value, f, bias)

    def own_lines(index, carry):
        for n in range(slots):
            own_line(index * slots + n, bias_of(index))
        return carry

    lax.fori_loop(0, planes // slots, own_lines, 0)

    def near_line(t):
        return lambda e, f, plane: near_ref[f, plane, t + e]

    def near_around(n):
        return lambda e, f, plane: around_ref[n, e, f, plane]

    def own(near, first):
        return jnp.stack([near(2, 2, first * slots + slot) for slot in range(slots)])

    zero = jnp.zeros((slots, 8, width), jnp.float32)
    def flow(x, near, low_e, high_e, sums, moments):
        own_x = own(near, 0)
        own_y = own(near, 1)
        if not moments:
            own_vx = own(near, 2)
            own_vy = own(near, 3)

        def along(e, sums):
            sums = list(sums)
            base_x = own_x - CELL * jnp.asarray(e - 2, jnp.float32)
            for f in range(5):
                for b in range(slots):
                    dx = near(e, f, b)[None] - base_x
                    dy = near(e, f, slots + b)[None] - own_y
                    square = dx * dx + dy * dy
                    inverse = lax.rsqrt(square)
                    dist = lax.rsqrt(inverse * inverse)
                    u = jnp.maximum(REACH - dist, 0.0)
                    slope = (u * u) * (near(e, f, 4 * slots + b)[None] * u)
                    slopes_ref[x * 5 + e, f, b] = slope
                    sums[0] = sums[0] + slope
                    sums[1] = sums[1] + slope * (dist - square)
                    if moments:
                        moment_ref[0, x * 5 + e, f, b] = slope * dx
                        moment_ref[1, x * 5 + e, f, b] = slope * dy
                    else:
                        dvx = near(e, f, 2 * slots + b)[None] - own_vx
                        dvy = near(e, f, 3 * slots + b)[None] - own_vy
                        sums[2] = sums[2] + slope * (dvx * dx + dvy * dy)
            return tuple(sums)

        return lax.fori_loop(low_e, high_e, along, sums)

    def stir(x, near):
        def along(e, sums):
            flux, sum_x, sum_y = sums
            for f in range(5):
                for b in range(slots):
                    moment_x = moment_ref[0, x * 5 + e, f, b]
                    moment_y = moment_ref[1, x * 5 + e, f, b]
                    flux = flux + moment_x * near(e, f, 2 * slots + b)[None]
                    flux = flux + moment_y * near(e, f, 3 * slots + b)[None]
                    sum_x = sum_x + moment_x
                    sum_y = sum_y + moment_y
            return flux, sum_x, sum_y

        flux, sum_x, sum_y = lax.fori_loop(0, 5, along, (zero,) * 3)
        own_ref[moment_at, x] = sum_x
        own_ref[moment_at + 1, x] = sum_y
        return flux - own(near, 2) * sum_x - own(near, 3) * sum_y

    def save(x, sums):
        for n, value in enumerate(sums):
            own_ref[n, x] = value

    def saved(x, count):
        return tuple(own_ref[n, x] for n in range(count))

    def each(first, last, work):
        def body(x, carry):
            work(x)
            return carry

        lax.fori_loop(first, last, body, 0)

    def flow_inner(t):
        low_e = jnp.maximum(0, 2 - t)
        high_e = jnp.minimum(5, steps + 2 - t)
        save(t, flow(t, near_line(t), low_e, high_e, (zero,) * 2, True))

    def flow_outer(index):
        t = index + (index // 2) * (steps - 4)
        low_e = jnp.where(t < 2, 0, steps + 2 - t)
        high_e = jnp.where(t < 2, 2 - t, 5)
        save(t, flow(t, near_line(t), low_e, high_e, saved(t, 2), True))

    def greet_and_flow(t):
        @pl.when(t == EARLY)
        def _():
            tall = 1 + jnp.where(my_row > 0, 1, 0) + jnp.where(my_row + 1 < rows, 1, 0)
            wide = 1 + jnp.where(my_col > 0, 1, 0) + jnp.where(my_col + 1 < cols, 1, 0)
            pl.semaphore_wait(barrier, tall * wide - 1)
            for way in (4, 5, 6, 7, 2, 3, 0, 1):

                @pl.when(exists(*DIRECTIONS[way]))
                def _(way=way):
                    copy(way).start()

        flow_inner(t)

    each(0, steps, greet_and_flow)


    for way in range(8):
        dr, dc = DIRECTIONS[way]

        @pl.when(exists(-dr, -dc))
        def _(way=way):
            copy(way).wait_recv()

    def ring(plane, top, bottom, bias):
        for f in range(5):
            above, below = shifted(top, f, bias), shifted(bottom, f, bias)
            first, second = near_ref[f, plane, 2], near_ref[f, plane, 3]
            before, last = near_ref[f, plane, steps], near_ref[f, plane, steps + 1]
            near_ref[f, plane, 0] = jnp.where(line == 0, under(above, 2), under(before, 1))
            near_ref[f, plane, 1] = jnp.where(line == 0, under(above, 1), under(last, 1))
            near_ref[f, plane, steps + 2] = jnp.where(line == 7, under(below, 7), under(first, 7))
            near_ref[f, plane, steps + 3] = jnp.where(line == 7, under(below, 6), under(second, 7))
            around_ref[2, 0, f, plane] = under(above, 2)
            around_ref[2, 1, f, plane] = under(above, 1)
            around_ref[2, 2, f, plane] = above
            around_ref[2, 3, f, plane] = jnp.where(line == 7, under(first, 7), under(above, 7))
            beyond = jnp.where(line == 7, under(second, 7), under(above, 6))
            around_ref[2, 4, f, plane] = jnp.where(line == 6, under(first, 6), beyond)
            beyond = jnp.where(line == 1, under(last, 2), under(below, 2))
            around_ref[3, 0, f, plane] = jnp.where(line == 0, under(before, 1), beyond)
            around_ref[3, 1, f, plane] = jnp.where(line == 0, under(last, 1), under(below, 1))
            around_ref[3, 2, f, plane] = below
            around_ref[3, 3, f, plane] = under(below, 7)
            around_ref[3, 4, f, plane] = under(below, 6)

    def widen(plane, inner, outer, bias):
        for f in range(5):
            mine = (lane + (span + 2 - f)) % span < span // 2
            here = shifted(jnp.where(mine, *inner), f, bias)
            bend = shifted(jnp.where(mine, *outer), f, bias)
            after = jnp.where(lane >= width - span, bend, lane_roll(here, -span))
            ahead = jnp.where(lane < span, bend, lane_roll(here, span))
            for n, value, up, down in ((0, here, after, ahead), (1, bend, here, here)):
                around_ref[n, 0, f, plane] = under(jnp.where(line >= 6, down, value), 2)
                around_ref[n, 1, f, plane] = under(jnp.where(line >= 7, down, value), 1)
                around_ref[n, 2, f, plane] = value
                around_ref[n, 3, f, plane] = under(jnp.where(line < 1, up, value), 7)
                around_ref[n, 4, f, plane] = under(jnp.where(line < 2, up, value), 6)

    def fold(top, bottom):
        return jnp.where(block == 0, top, lane_roll(bottom, span * (steps - 1)))

    def arrive(plane, g, n, bias):
        top, bottom = above_ref[0, plane], above_ref[1, plane]
        ring(plane, top, bottom, bias)

        def strips(mine, theirs):
            left = lane_roll(jnp.where(left_half, mine, theirs), 6)
            right = lane_roll(jnp.where(left_half, theirs, mine), 10)
            return left, right

        inner = jnp.where(left_half, beside_ref[1, plane], beside_ref[0, plane])
        ends = [jnp.where(left_half, corner_ref[1, level, g], corner_ref[0, level, g]) for level in (0, 1)]
        outer = fold(lane_roll(ends[0], -span * n), lane_roll(ends[1], -span * n))
        widen(plane, strips(edge_ref[plane], inner), strips(fold(top, bottom), outer), bias)

    def arrive_some(index, carry):
        g = index // 2
        for half in range(2):

            @pl.when(index % 2 == half)
            def _(half=half):
                for n in range(slots):
                    arrive(index * slots + n, g, half * slots + n, bias_of(index))

        return carry

    lax.fori_loop(0, planes // slots, arrive_some, 0)

    each(0, 4, flow_outer)
    save(strip, flow(strip, near_around(0), 0, 5, (zero,) * 2, True))
    each(1, 4, lambda n: save(steps + n, flow(steps + n, near_around(n), 0, 5, (zero,) * 3, False)))

    full = (8, width)
    low = jnp.broadcast_to(low_ref[0], full)
    high = jnp.broadcast_to(high_ref[0], full)
    middle = 0.5 * (high + low)
    radius = 0.5 * (high - low)
    quotient = middle / radius
    factor_zero = 1.0 / quotient
    factor_one = 1.0 / (2.0 * quotient - factor_zero)
    factor_two = 1.0 / (2.0 * quotient - factor_one)
    over_middle = 1.0 / middle
    keep_one = factor_one * factor_zero
    keep_two = factor_two * factor_one
    gain_one = 2.0 * factor_one / radius
    gain_two = 2.0 * factor_two / radius

    def everyone(work):
        each(0, steps, lambda t: work(t, near_line(t)))
        each(0, 4, lambda n: work(steps + n, near_around(n)))

    def first_step(x, slope_sum, dens, inflow):
        density = BACKGROUND + (KERNEL_NORM / SLOPE_NORM) * (slope_sum + (4.0 / REACH**2) * dens)
        inverse = 1.0 / density
        source = inflow * inverse * (-1.0 / (CELL * TIME_STEP))
        own_ref[inverse_at, x] = inverse
        own_ref[diagonal_at, x] = DIAGONAL_SHIFT + 2.0 * inverse * slope_sum
        own_ref[residual_at, x] = source
        own_ref[sum_at, x] = source * over_middle[None]

    def turn(value):
        return jnp.where(left_half, lane_roll(value, -2), lane_roll(value, 2))

    def mend(value, turned, s):
        outermost = (lane < 2) | (lane >= width - 2)
        return jnp.where(outermost, lane_roll(turned, -span * s - span // 2), value)

    def refresh(at):
        for slot in range(slots):
            for t in range(steps):
                tile_ref[slot, pl.ds(t, 8, stride=8), :] = own_ref[at, t, slot]
            inner, outer = own_ref[at, strip, slot], own_ref[at, corners, slot]
            turned = turn(inner)
            for s in range(steps):
                window = slice(8 * s, 8 * s + 8)
                tile_ref[slot, window, :] = mend(tile_ref[slot, window, :], turned, s)
            turned = turn(outer)
            top = mend(own_ref[at, tops, slot], turned, 0)
            bottom = mend(own_ref[at, tops + 1, slot], turned, steps - 1)
            own_line(slot, None)
            ring(slot, top, bottom, None)

            def strips(value, mine):
                left = jnp.where(left_half, value, lane_roll(mine, 6))
                right = jnp.where(left_half, lane_roll(mine, 10), value)
                return left, right

            widen(slot, strips(inner, edges(slot)), strips(outer, fold(top, bottom)), None)

    def gather(x, near):
        def along(e, totals):
            totals = list(totals)
            for f in range(5):
                for b in range(slots):
                    value = near(e, f, b)[None]
                    totals[b % 2] = totals[b % 2] + slopes_ref[x * 5 + e, f, b] * value
            return tuple(totals)

        even, odd = lax.fori_loop(0, 5, along, (zero, zero))
        return even + odd

    def improve(x, near, here):
        total = gather(x, near)
        change = own_ref[diagonal_at, x] * here - 2.0 * own_ref[inverse_at, x] * total
        residual = own_ref[residual_at, x] - change
        own_ref[residual_at, x] = residual
        return residual

    def second_step(x, near):
        here = own_ref[sum_at, x]
        own_ref[step_at, x] = keep_one[None] * here + gain_one[None] * improve(x, near, here)

    def third_step(x, near):
        here = own_ref[step_at, x]
        third = keep_two[None] * here + gain_two[None] * improve(x, near, here)
        own_ref[sum_at, x] = own_ref[sum_at, x] + here + third

    def push(x, near):
        def along(e, totals):
            push_x, push_y = totals
            for f in range(5):
                for b in range(slots):
                    value = near(e, f, b)[None]
                    push_x = push_x + moment_ref[0, x * 5 + e, f, b] * value
                    push_y = push_y + moment_ref[1, x * 5 + e, f, b] * value
            return push_x, push_y

        pushes = lax.fori_loop(0, 5, along, (zero, zero))
        solved = own_ref[sum_at, x]
        scale = own_ref[inverse_at, x] * (TIME_STEP / CELL)
        return [
            own(near, 2 + axis) - scale * (pushes[axis] - solved * own_ref[moment_at + axis, x])
            for axis in range(2)
        ]

    def kick_line(t):
        for axis, value in enumerate(push(t, near_line(t))):
            for slot in range(slots):
                nv_ref[axis, slot, pl.ds(t, 8, stride=8), :] = value[slot]

    def kick_ends():
        turned = [[turn(value[slot]) for slot in range(slots)] for value in push(strip, near_around(0))]
        for s in range(steps):
            window = slice(8 * s, 8 * s + 8)
            live = counts_ref[window, :]
            for slot in range(slots):
                occupied = jnp.where(live > slot, 1.0, 0.0).astype(jnp.float32)
                for axis in range(2):
                    value = mend(nv_ref[axis, slot, window, :], turned[axis][slot], s)
                    nv_ref[axis, slot, window, :] = occupied * value
                press_ref[slot, window, :] = occupied * tile_ref[slot, window, :]

    for way in range(8):

        @pl.when(exists(*DIRECTIONS[way]))
        def _(way=way):
            copy(way).wait_send()

    each(0, steps, lambda t: first_step(t, *saved(t, 2), stir(t, near_line(t))))
    first_step(strip, *saved(strip, 2), stir(strip, near_around(0)))
    each(1, 4, lambda n: first_step(steps + n, *saved(steps + n, 3)))
    refresh(sum_at)
    everyone(second_step)
    refresh(step_at)
    everyone(third_step)
    refresh(sum_at)
    each(0, steps, kick_line)
    kick_ends()

def on_device(rows, cols, offsets, velocity, mass, counts, spectrum_low, spectrum_high):
    slots, height, width = mass.shape
    steps = height // 8
    span = width // steps
    assert height % 8 == 0 and steps == 8 and width % 128 == 0 and span == 16
    planes = 5 * slots
    bends = -(-planes * span // width)
    count = steps + 4
    room_out = 4 * (velocity.size + mass.size)
    vmem = pl.BlockSpec(memory_space=pltpu.VMEM)
    hbm = pl.BlockSpec(memory_space=pltpu.HBM)

    def room(*shape):
        return pltpu.VMEM(shape, jnp.float32)

    results = pl.pallas_call(
        functools.partial(kernel, rows, cols),
        out_shape=(
            pltpu.VMEM(velocity.shape, jnp.float32),
            pltpu.VMEM(mass.shape, jnp.float32),
        ),
        in_specs=[hbm] * 6,
        out_specs=(vmem, vmem),
        scratch_shapes=[
            room(*offsets.shape),
            room(*velocity.shape),
            room(*mass.shape),
            pltpu.VMEM(counts.shape, jnp.int32),
            pltpu.SMEM(spectrum_low.shape, jnp.float32),
            pltpu.SMEM(spectrum_high.shape, jnp.float32),
            pltpu.SemaphoreType.DMA((6,)),
            room(planes, height, width),
            room(2, planes, 8, width),
            room(planes, 8, width),
            room(2, planes, 8, width),
            room(2, bends, 8, width),
            room(2, 2, bends, 8, width),
            room(5, planes, steps + 4, 8, width),
            room(4, 5, 5, planes, 8, width),
            room(count * 5, 5, slots, slots, 8, width),
            room(2, (steps + 1) * 5, 5, slots, slots, 8, width),
            room(7, count, slots, 8, width),
            pltpu.SemaphoreType.DMA((8,)),
            pltpu.SemaphoreType.DMA((8,)),
        ],
        compiler_params=pltpu.CompilerParams(
            collective_id=0,
            has_side_effects=True,
            vmem_limit_bytes=VMEM_BYTES - room_out - SPARE,
        ),
        name="sph_step",
    )(offsets, velocity, mass, counts, spectrum_low, spectrum_high)
    return pl.pallas_call(
        put_out,
        out_shape=(
            jax.ShapeDtypeStruct(velocity.shape, jnp.float32),
            jax.ShapeDtypeStruct(mass.shape, jnp.float32),
        ),
        in_specs=[vmem] * 2,
        out_specs=(hbm, hbm),
        scratch_shapes=[pltpu.SemaphoreType.DMA((2,))],
        compiler_params=pltpu.CompilerParams(vmem_limit_bytes=1 << 20),
        name="put_out",
    )(*results)


def put_out(nv_ref, press_ref, nv_hbm, press_hbm, sem):
    copies = [
        pltpu.make_async_copy(nv_ref, nv_hbm, sem.at[0]),
        pltpu.make_async_copy(press_ref, press_hbm, sem.at[1]),
    ]
    for copy in copies:
        copy.start()
    for copy in copies:
        copy.wait()


def solution(mesh):
    placed = (
        P(None, None, "row", "col"),
        P(None, None, "row", "col"),
        P(None, "row", "col"),
        P("row", "col"),
        P(),
        P(),
    )
    return jax.shard_map(
        functools.partial(on_device, mesh.shape["row"], mesh.shape["col"]),
        mesh=mesh,
        in_specs=placed,
        out_specs=(P(None, None, "row", "col"), P(None, "row", "col")),
        check_vma=False,
    )
```
